32 devices in a mesh: tm: 4 (over z), space: 2 (over y), clip: 4 (over x, core).
Axes of the slice: x: 2, y: 2, z: 4, core: 2. Of those that a mesh axis runs over, the one named last changes fastest.
Arguments:
- activations: bfloat16 [96, 64, 1408], P(('clip', 'tm'), 'space'), parts along dimension 0, may hold values from -200 to 200
- attn_gain: float32 [1408], replicated, may hold values from 0.5 to 2
- attn_shift: float32 [1408], replicated, may hold values from -3 to 3
- w_qkv: bfloat16 [1408, 4224], replicated, may hold values from -4 to 4
- b_qkv: float32 [4224], replicated, may hold values from -3 to 3
- w_out: bfloat16 [1408, 1408], replicated, may hold values from -2.5 to 2.5
- b_out: float32 [1408], replicated, may hold values from -3 to 3
- final_gain: float32 [1408], replicated, may hold values from 0.5 to 2
- final_shift: float32 [1408], replicated, may hold values from -3 to 3
- mask_tokens: int32 [32, 192], P('clip'), parts along dimension 0, may hold values from -1 to 1535, as said below
- assignment: int32 [32], P('clip'), parts along dimension 0, may hold values from 0 to 7, each once
Outputs:
- targets: bfloat16 [32, 192, 1408], P(('clip', 'tm', 'space')), parts along dimension 0
The draws below stay inside these ranges and needn't reach their ends.
There are 4 independent parts, one for each index of `clip`. The reference program is written for one: setup_inputs(seed, part) draws one part's arguments, and reference() takes and returns one part's arrays. A program takes and returns all parts, laid end to end along the dimension named above; an argument that names none is the same for every part. Nothing has to cross between parts.
Inputs may be any that keep to these rules, and one draw needn't show every extreme that they name: `mask_tokens`: each row lists distinct tokens, no token in two rows; its listed entries come first in no fixed order, then -1 to the end. The block of tokens of one device (temporal positions k * 6 to k * 6 + 5 and patch positions m * 32 to m * 32 + 31) gives at most 24 entries to one row; in some row every such block gives exactly 24, so that row is full. `assignment`: each owner once.
All inputs are finite; a program needn't handle non-finite values.
Results may differ from the reference program's by a relative error of at most 0.0085.
The reference program's roundings to bfloat16 on the way (of `normed_in`, `projected`, `rounded`, `attended`, `hidden` and `normed`) count: a program that leaves them out, or rounds other values in their place, can miss the bound.
Values may be sent and summed in bfloat16 or wider, within the bound.
A program may use at most 128 MiB of HBM per device.

```python
import math
import jax
import jax.numpy as jnp
from jax import lax

D = 1408
HEADS = 16
HD = 88
T_DEV = 6
S_DEV = 32
TEMPORAL = 24
SPATIAL = 64
TOK_DEV = 192
TOKENS = 1536
OWNERS = 8
SRC_CAP = 24
CAP = 192


def draw_activations(key, part):
    noise_key = jax.random.fold_in(key, 0)
    drawn = jnp.clip(jax.random.normal(noise_key, (TOKENS, D), jnp.float32), -6.0, 6.0)
    return drawn.reshape(TEMPORAL, SPATIAL, D).astype(jnp.bfloat16)


def draw_w_qkv(key, part):
    second_key = jax.random.fold_in(key, 1)
    third_key = jax.random.fold_in(key, 2)
    query_key_part = jnp.clip(jax.random.normal(second_key, (D, 2 * D), jnp.float32), -6.0, 6.0) * math.sqrt(1.5 / D)
    value_part = jnp.clip(jax.random.normal(third_key, (D, D), jnp.float32), -6.0, 6.0) / math.sqrt(D)
    return jnp.concatenate((query_key_part, value_part), axis=1).astype(jnp.bfloat16)


def pick_order(source_seed):
    return jax.random.permutation(source_seed, TOK_DEV)


def pick_rank(owner_seed):
    return jax.random.permutation(owner_seed, CAP)


def draw_mask_tokens(key, part):
    count_key, full_key, source_key, order_key = jax.random.split(key, 4)
    spaces = SPATIAL // S_DEV
    counts = jax.random.randint(count_key, (OWNERS, OWNERS), 0, SRC_CAP + 1)
    full_owner = jax.random.randint(full_key, (), 0, OWNERS)
    counts = jnp.where(jnp.arange(OWNERS)[:, None] == full_owner, SRC_CAP, counts)
    starts = jnp.cumsum(counts, axis=0) - counts
    orders = jax.vmap(pick_order)(jax.random.split(source_key, OWNERS))
    slots = jnp.arange(SRC_CAP)
    positions = jnp.minimum(starts[:, :, None] + slots[None, None, :], TOK_DEV - 1)
    sources = jnp.broadcast_to(jnp.arange(OWNERS)[None, :, None], positions.shape)
    local_rows = orders[sources, positions]
    frames = sources // spaces * T_DEV + local_rows // S_DEV
    patches = sources % spaces * S_DEV + local_rows % S_DEV
    token_ids = (frames * SPATIAL + patches).reshape(OWNERS, CAP)
    listed = (slots[None, None, :] < counts[:, :, None]).reshape(OWNERS, CAP)
    ranks = jax.vmap(pick_rank)(jax.random.split(order_key, OWNERS))
    sort_keys = jnp.where(listed, ranks, CAP + jnp.arange(CAP)[None, :])
    new_order = jnp.argsort(sort_keys, axis=1, stable=True)
    token_ids = jnp.take_along_axis(token_ids, new_order, axis=1)
    listed = jnp.take_along_axis(listed, new_order, axis=1)
    return jnp.where(listed, token_ids, -1).astype(jnp.int32)


def scatter_about(stream_key, dims, scale, most, dtype=jnp.bfloat16):
    result = jax.random.normal(stream_key, dims, jnp.float32) * scale
    return jnp.minimum(jnp.maximum(result, -most), most).astype(dtype)


def setup_inputs(seed: int = 0, part: int = 0) -> dict:
    splits = jax.random.split(jax.random.key(seed), 12)
    own_keys = jax.random.split(jax.random.fold_in(splits[11], part), 12)
    return {
        "activations": draw_activations(jax.random.fold_in(jax.random.fold_in(splits[11], part), 71), part),
        "attn_gain": jnp.clip(jnp.exp(jax.random.uniform(splits[1], (D,), jnp.float32, math.log(0.5), math.log(2.0))), 0.5, 2.0),
        "attn_shift": scatter_about(splits[2], (D,), 0.5, 3.0, jnp.float32),
        "w_qkv": draw_w_qkv(jax.random.fold_in(splits[11], 71), part),
        "b_qkv": scatter_about(splits[4], (3 * D,), 0.5, 3.0, jnp.float32),
        "w_out": scatter_about(splits[5], (D, D), (max(D // 256, 1)) ** -0.5, 2.5),
        "b_out": scatter_about(splits[6], (D,), 0.5, 3.0, jnp.float32),
        "final_gain": jnp.clip(jnp.exp(jax.random.uniform(splits[7], (D,), jnp.float32, math.log(0.5), math.log(2.0))), 0.5, 2.0),
        "final_shift": scatter_about(splits[8], (D,), 0.5, 3.0, jnp.float32),
        "mask_tokens": draw_mask_tokens(jax.random.fold_in(jax.random.fold_in(splits[11], part), 71), part),
        "assignment": jax.random.permutation(own_keys[10], OWNERS).astype(jnp.int32),
    }


EPSILON = 1e-06

def layer_norm(values, ln_gain, ln_shift):
    centre = lax.optimization_barrier(jnp.mean(values, axis=-1, keepdims=True))
    deviation = values - centre
    variance = lax.optimization_barrier(jnp.mean(deviation * deviation, axis=-1, keepdims=True))
    return deviation * lax.rsqrt(variance + EPSILON) * ln_gain + ln_shift

def reference(activations, attn_gain, attn_shift, w_qkv, b_qkv, w_out, b_out, final_gain, final_shift, mask_tokens, assignment):
    tokens_flat = activations.reshape(TOKENS, D)
    normed_in = layer_norm(tokens_flat.astype(jnp.float32), attn_gain, attn_shift).astype(jnp.bfloat16)
    projected = (jnp.dot(normed_in, w_qkv, preferred_element_type=jnp.float32) + b_qkv).astype(jnp.bfloat16)
    query_blocks = projected[:, :D].reshape(TOKENS // TOK_DEV, TOK_DEV, HEADS, HD)
    key_rows = projected[:, D:2 * D].reshape(TOKENS, HEADS, HD).astype(jnp.float32)
    value_rows = projected[:, 2 * D:].reshape(TOKENS, HEADS, HD).astype(jnp.float32)
    score_scale = 1.0 / math.sqrt(HD)

    def attend_block(query_block):
        scores = jnp.einsum('qhe,khe->hqk', query_block.astype(jnp.float32), key_rows) * score_scale
        highest = lax.optimization_barrier(jnp.max(scores, axis=-1, keepdims=True))
        weights = jnp.exp(scores - highest)
        totals = lax.optimization_barrier(jnp.sum(weights, axis=-1))
        rounded = lax.optimization_barrier(weights.astype(jnp.bfloat16))
        weighted = jnp.einsum('hqk,khe->hqe', rounded.astype(jnp.float32), value_rows)
        return jnp.transpose(weighted / totals[:, :, None], (1, 0, 2)).astype(jnp.bfloat16)
    attended = lax.map(attend_block, query_blocks).reshape(TOKENS, D)
    projected_out = jnp.dot(attended, w_out, preferred_element_type=jnp.float32)
    hidden = (tokens_flat.astype(jnp.float32) + projected_out + b_out).astype(jnp.bfloat16)
    normed = layer_norm(hidden.astype(jnp.float32), final_gain, final_shift).astype(jnp.bfloat16)
    owner_lists = jnp.take(mask_tokens, assignment, axis=0)
    picked = jnp.take(normed, jnp.maximum(owner_lists, 0), axis=0)
    return jnp.where((owner_lists >= 0)[:, :, None], picked, jnp.zeros_like(picked))
```

```python
import functools
import math

import jax
import jax.numpy as jnp
import numpy as np
from jax import lax
from jax.experimental import pallas as pl
from jax.experimental.pallas import tpu as pltpu
from jax.sharding import PartitionSpec as P

HEADS = 16


EPSILON = 1e-06
FLOOR_SCORE = -1e30


def layer_norm(values, ln_gain, ln_shift):
    centre = jnp.mean(values, axis=-1, keepdims=True)
    deviation = values - centre
    variance = jnp.mean(deviation * deviation, axis=-1, keepdims=True)
    return deviation * lax.rsqrt(variance + EPSILON) * ln_gain + ln_shift


def start_state(query_heads):
    query_count, head_count, head_width = query_heads.shape
    return (
        jnp.full((head_count, query_count), FLOOR_SCORE, jnp.float32),
        jnp.zeros((head_count, query_count), jnp.float32),
        jnp.zeros((head_count, query_count, head_width), jnp.float32),
    )


def finish_state(carried_state):
    running_max, running_total, running_sum = carried_state
    return jnp.transpose(running_sum / running_total[:, :, None], (1, 0, 2)).astype(jnp.bfloat16)


def make_attend(query_heads):
    query_count, head_count, head_width = query_heads.shape
    score_scale = 1.0 / math.sqrt(head_width)

    def one_block(carried_state, kv_block):
        running_max, running_total, running_sum = carried_state
        block_length = kv_block.shape[1]
        key_rows = kv_block[0].reshape(block_length, head_count, head_width)
        value_rows = kv_block[1].reshape(block_length, head_count, head_width)
        scores = (
            jnp.einsum("qhe,khe->hqk", query_heads, key_rows, preferred_element_type=jnp.float32)
            * score_scale
        )
        new_max = jnp.maximum(running_max, jnp.max(scores, axis=-1))
        factor = jnp.exp(running_max - new_max)
        weights = jnp.exp(scores - new_max[:, :, None])
        running_total = running_total * factor + jnp.sum(weights, axis=-1)
        running_sum = running_sum * factor[:, :, None] + jnp.einsum(
            "hqk,khe->hqe",
            weights.astype(jnp.bfloat16),
            value_rows,
            preferred_element_type=jnp.float32,
        )
        return (new_max, running_total, running_sum)

    def attend(carried_state, key_piece, first_row):
        length = key_piece.shape[1]
        block_rows = length
        while block_rows > 1024 and block_rows % 2 == 0:
            block_rows = block_rows // 2

        def advance(position, carried):
            kv_block = lax.dynamic_slice_in_dim(key_piece, position * block_rows, block_rows, 1)
            return one_block(carried, kv_block)

        return lax.fori_loop(0, length // block_rows, advance, carried_state)

    return attend


def local(
    activations,
    attn_gain,
    attn_shift,
    w_qkv,
    b_qkv,
    w_out,
    b_out,
    final_gain,
    final_shift,
    mask_tokens,
    assignment,
):
    frame_count, patch_count, model_width = activations.shape
    local_rows = frame_count * patch_count
    head_width = model_width // HEADS
    tokens_flat = activations.reshape(local_rows, model_width)
    normed_in = layer_norm(tokens_flat.astype(jnp.float32), attn_gain, attn_shift).astype(
        jnp.bfloat16
    )
    projected = (jnp.dot(normed_in, w_qkv, preferred_element_type=jnp.float32) + b_qkv).astype(
        jnp.bfloat16
    )
    query_rows = projected[:, :model_width]
    paired = jnp.stack(
        (projected[:, model_width : 2 * model_width], projected[:, 2 * model_width :])
    )
    groups = lax.axis_size("space")
    group_heads = HEADS // groups
    stacked = jnp.stack((query_rows, paired[0], paired[1])).reshape(
        3, local_rows, groups, group_heads, head_width
    )
    swapped = lax.all_to_all(stacked, "space", split_axis=2, concat_axis=1, tiled=True)
    gathered_rows = swapped.shape[1]
    kept_heads = swapped.shape[3]
    query_heads = swapped[0].reshape(gathered_rows, kept_heads, head_width)
    kv_rows = swapped[1:].reshape(2, gathered_rows, kept_heads * head_width)
    time_state = make_attend(query_heads)(
        start_state(query_heads), lax.all_gather(kv_rows, "tm", axis=1, tiled=True), jnp.int32(0)
    )
    head_output = finish_state(time_state).reshape(gathered_rows, 1, kept_heads, head_width)
    merged = lax.all_to_all(head_output, "space", split_axis=0, concat_axis=1, tiled=True)
    attended = merged.reshape(local_rows, model_width)
    hidden = (
        tokens_flat.astype(jnp.float32)
        + jnp.dot(attended, w_out, preferred_element_type=jnp.float32)
        + b_out
    ).astype(jnp.bfloat16)
    normed = layer_norm(hidden.astype(jnp.float32), final_gain, final_shift).astype(jnp.bfloat16)
    owners = mask_tokens.shape[0]
    capacity = mask_tokens.shape[1]
    per_source = capacity // owners
    spaces = lax.axis_size("space")
    spatial = patch_count * spaces
    own_index = lax.axis_index("tm") * spaces + lax.axis_index("space")
    owner_lists = jnp.take(mask_tokens, assignment, axis=0)
    listed = owner_lists >= 0
    clipped = jnp.maximum(owner_lists, 0)
    token_frame = clipped // spatial
    token_patch = clipped % spatial
    home_device = token_frame // frame_count * spaces + token_patch // patch_count
    local_row = token_frame % frame_count * patch_count + token_patch % patch_count
    mine = listed & (home_device == own_index)
    slot_index = jnp.cumsum(mine.astype(jnp.int32), axis=1) - 1
    wanted = mine[:, None, :] & (
        slot_index[:, None, :] == jnp.arange(per_source, dtype=jnp.int32)[None, :, None]
    )
    picks = jnp.sum(jnp.where(wanted, local_row[:, None, :], 0), axis=-1)
    present = jnp.any(wanted, axis=-1)
    own_home = lax.dynamic_index_in_dim(home_device, own_index, 0, keepdims=False)
    own_listed = lax.dynamic_index_in_dim(listed, own_index, 0, keepdims=False)
    entry_order = jnp.arange(capacity, dtype=jnp.int32)
    earlier = (
        (entry_order[:, None] < entry_order[None, :])
        & own_listed[:, None]
        & (own_home[:, None] == own_home[None, :])
    )
    entry_rank = jnp.sum(earlier.astype(jnp.int32), axis=0)
    where_from = jnp.where(own_listed, own_home * per_source + entry_rank, 0)
    outgoing = jnp.where(
        present[:, :, None], jnp.take(normed, picks, axis=0), jnp.zeros((), jnp.bfloat16)
    )
    arrived = lax.all_to_all(outgoing, ("tm", "space"), split_axis=0, concat_axis=0, tiled=True)
    row_table = arrived.reshape(owners * per_source, model_width)
    placed = jnp.take(row_table, where_from, axis=0)
    return jnp.where(own_listed[:, None], placed, jnp.zeros((), jnp.bfloat16))[None]


LANES = 128
WINDOW = 256
VMEM_LIMIT = 60 * 1024 * 1024
MESH = pl.DeviceIdType.MESH


def norm_rows(values, gain, shift):
    return layer_norm(values.astype(jnp.float32), gain, shift).astype(jnp.bfloat16)


def fused_kernel(
    times,
    head_width,
    x_ref,
    gain_ref,
    shift_ref,
    w_qkv_ref,
    b_qkv_ref,
    w_out_ref,
    b_out_ref,
    final_gain_ref,
    final_shift_ref,
    lists_ref,
    assignment_ref,
    columns_ref,
    out_ref,
    x_all,
    kv_all,
    w_qkv,
    w_out,
    normed,
    queries,
    attended,
    local_sem,
    up_send,
    down_send,
    side_send,
    line_recv,
    side_recv,
):
    me = lax.axis_index("tm")
    side = lax.axis_index("space")
    other = 1 - side
    rows, width = x_ref.shape
    load_x = pltpu.make_async_copy(x_ref, x_all.at[me, side], local_sem.at[0])
    load_qkv = pltpu.make_async_copy(w_qkv_ref, w_qkv, local_sem.at[1])
    load_out = pltpu.make_async_copy(w_out_ref, w_out, local_sem.at[2])
    load_x.start()
    load_qkv.start()
    load_out.start()

    has_up = me < times - 1
    has_down = me > 0

    barrier = pltpu.get_barrier_semaphore()
    pl.semaphore_signal(barrier, inc=1, device_id={"space": other}, device_id_type=MESH)

    @pl.when(has_up)
    def _():
        pl.semaphore_signal(barrier, inc=1, device_id={"tm": me + 1}, device_id_type=MESH)

    @pl.when(has_down)
    def _():
        pl.semaphore_signal(barrier, inc=1, device_id={"tm": me - 1}, device_id_type=MESH)

    pl.semaphore_wait(barrier, 1 + has_up.astype(jnp.int32) + has_down.astype(jnp.int32))

    def up_copy(source, block):
        return pltpu.make_async_remote_copy(
            source, x_all.at[block, side], up_send.at[block], line_recv.at[block],
            device_id={"tm": me + 1}, device_id_type=MESH,
        )

    def down_copy(source, block):
        return pltpu.make_async_remote_copy(
            source, x_all.at[block, side], down_send.at[block], line_recv.at[block],
            device_id={"tm": me - 1}, device_id_type=MESH,
        )

    def side_copy(source, block, from_side):
        return pltpu.make_async_remote_copy(
            source, x_all.at[block, from_side], side_send.at[block], side_recv.at[block],
            device_id={"space": other}, device_id_type=MESH,
        )

    @pl.when(has_up)
    def _():
        up_copy(x_ref, me).start()

    @pl.when(has_down)
    def _():
        down_copy(x_ref, me).start()

    side_copy(x_ref, me, side).start()

    def arrive_and_forward(step):
        below, above = me - step, me + step

        @pl.when(below >= 0)
        def _():
            held = x_all.at[below, side]
            up_copy(held, below).wait_recv()

            @pl.when(has_up)
            def _():
                up_copy(held, below).start()

            side_copy(held, below, side).start()

        @pl.when(above < times)
        def _():
            held = x_all.at[above, side]
            down_copy(held, above).wait_recv()

            @pl.when(has_down)
            def _():
                down_copy(held, above).start()

            side_copy(held, above, side).start()

    reach = jnp.minimum(me, times - 1 - me)

    def ordered(place):
        if place == 0:
            return me
        near = me - (place + 1) // 2 if place % 2 else me + place // 2
        far_step = place - reach
        far = jnp.where(2 * me > times - 1, me - far_step, me + far_step)
        return jnp.where(place <= 2 * reach, near, far)

    tiles = 2 * width // WINDOW

    def project(blocks):
        count = len(blocks)
        for place, (block, from_side) in enumerate(blocks):
            normed[place * rows : (place + 1) * rows, :] = norm_rows(
                x_all[block, from_side], gain_ref[...], shift_ref[...]
            )

        def one_tile(tile, carried):
            start = pl.multiple_of(tile * WINDOW, WINDOW)
            shifted = pl.multiple_of(width + tile * WINDOW, LANES)
            made = jnp.dot(
                normed[: count * rows, :],
                w_qkv[:, pl.ds(shifted, WINDOW)],
                preferred_element_type=jnp.float32,
            )
            made = (made + b_qkv_ref[:, pl.ds(shifted, WINDOW)]).astype(jnp.bfloat16)
            for place, (block, from_side) in enumerate(blocks):
                kv_all[block * 2 + from_side, :, pl.ds(start, WINDOW)] = made[
                    place * rows : (place + 1) * rows, :
                ]
            return carried

        lax.fori_loop(0, tiles, one_tile, 0)

    load_x.wait()
    load_qkv.wait()
    project([(me, side)])
    for step in range(1, times):
        arrive_and_forward(step)
        earlier = ordered(step - 1)
        side_copy(x_all.at[earlier, other], earlier, other).wait_recv()
        project([(ordered(step), side), (earlier, other)])
    last = ordered(times - 1)
    side_copy(x_all.at[last, other], last, other).wait_recv()
    project([(last, other)])

    own = (me * 2 + side).astype(jnp.float32)
    places = lax.broadcasted_iota(jnp.int32, assignment_ref.shape, 1).astype(jnp.float32)
    owner = jnp.sum(jnp.where(places == own, assignment_ref[...], 0.0), axis=1, keepdims=True)
    list_places = lax.broadcasted_iota(jnp.int32, lists_ref.shape, 0).astype(jnp.float32)
    token_row = jnp.sum(jnp.where(list_places == owner, lists_ref[...], 0.0), axis=0, keepdims=True)
    capacity = lists_ref.shape[1]
    diagonal = lax.broadcasted_iota(jnp.int32, (capacity, capacity), 0) == lax.broadcasted_iota(
        jnp.int32, (capacity, capacity), 1
    )
    tokens = jnp.sum(jnp.where(diagonal, token_row, 0.0), axis=1, keepdims=True)
    one_hot = (tokens == columns_ref[...]).astype(jnp.float32).astype(jnp.bfloat16)
    picked = jnp.dot(
        one_hot,
        x_all[...].reshape(times * 2 * rows, width),
        preferred_element_type=jnp.float32,
    )
    out_ref[0] = picked.astype(jnp.bfloat16)
    queries[...] = (
        jnp.dot(
            norm_rows(picked, gain_ref[...], shift_ref[...]),
            w_qkv[:, :width],
            preferred_element_type=jnp.float32,
        )
        + b_qkv_ref[:, :width]
    ).astype(jnp.bfloat16)
    attended[...] = jnp.zeros_like(attended)
    score_scale = math.log2(math.e) / math.sqrt(head_width)
    all_rows = times * 2 * rows

    def one_head(head, carried):
        first = head * head_width
        base = pl.multiple_of(jnp.minimum(first // LANES, width // LANES - 2) * LANES, LANES)
        value_base = pl.multiple_of(base + width, LANES)
        lane = lax.broadcasted_iota(jnp.int32, (capacity, WINDOW), 1) + base
        inside = (lane >= first) & (lane < first + head_width)
        query = jnp.where(inside, queries[:, pl.ds(base, WINDOW)].astype(jnp.float32), 0.0)
        keys = kv_all[:, :, pl.ds(base, WINDOW)].reshape(all_rows, WINDOW)
        values = kv_all[:, :, pl.ds(value_base, WINDOW)].reshape(all_rows, WINDOW)
        scores = (
            lax.dot_general(
                query.astype(jnp.bfloat16), keys, (((1,), (1,)), ((), ())),
                preferred_element_type=jnp.float32,
            )
            * score_scale
        )
        weights = jnp.exp2(scores - jnp.max(scores, axis=1, keepdims=True))
        totals = jnp.sum(weights, axis=1, keepdims=True)
        summed = jnp.dot(weights.astype(jnp.bfloat16), values, preferred_element_type=jnp.float32)
        attended[:, pl.ds(base, WINDOW)] += jnp.where(inside, summed / totals, 0.0)
        return carried

    lax.fori_loop(0, HEADS, one_head, 0)
    load_out.wait()
    hidden = (
        out_ref[0].astype(jnp.float32)
        + jnp.dot(
            attended[...].astype(jnp.bfloat16), w_out[...], preferred_element_type=jnp.float32
        )
        + b_out_ref[...]
    ).astype(jnp.bfloat16)
    final = layer_norm(hidden.astype(jnp.float32), final_gain_ref[...], final_shift_ref[...])
    out_ref[0] = jnp.where(tokens >= 0, final, 0.0).astype(jnp.bfloat16)

    for block in range(times):

        @pl.when(has_up & (block <= me))
        def _():
            up_copy(x_all.at[block, side], block).wait_send()

        @pl.when(has_down & (block >= me))
        def _():
            down_copy(x_all.at[block, side], block).wait_send()

        side_copy(x_all.at[block, side], block, side).wait_send()


def fits_fused(times, spaces, rows, width, capacity):
    all_rows = times * spaces * rows
    held = 2 * (all_rows * width * 3 + width * width * 4 + 2 * rows * width)
    held += 4 * capacity * (width * 2 + all_rows * 3)
    return (
        spaces == 2
        and held < VMEM_LIMIT
        and width % LANES == 0
        and width // HEADS <= LANES
        and rows % 16 == 0
    )


def fused_local(
    activations,
    attn_gain,
    attn_shift,
    w_qkv,
    b_qkv,
    w_out,
    b_out,
    final_gain,
    final_shift,
    mask_tokens,
    assignment,
):
    frames, patches, width = activations.shape
    rows = frames * patches
    times = lax.axis_size("tm")
    spaces = lax.axis_size("space")
    if not fits_fused(times, spaces, rows, width, mask_tokens.shape[1]):
        return local(
            activations, attn_gain, attn_shift, w_qkv, b_qkv, w_out, b_out,
            final_gain, final_shift, mask_tokens, assignment,
        )
    capacity = mask_tokens.shape[1]
    order = np.arange(times * frames * spaces * patches).reshape(times, frames, spaces, patches)
    columns = order.transpose(0, 2, 1, 3).reshape(1, -1).astype(np.float32)
    vmem = pl.BlockSpec(memory_space=pltpu.VMEM)
    hbm = pl.BlockSpec(memory_space=pl.ANY)
    return pl.pallas_call(
        functools.partial(fused_kernel, times, width // HEADS),
        out_shape=jax.ShapeDtypeStruct((1, capacity, width), jnp.bfloat16),
        in_specs=[vmem, vmem, vmem, hbm, vmem, hbm, vmem, vmem, vmem, vmem, vmem, vmem],
        out_specs=vmem,
        scratch_shapes=[
            pltpu.VMEM((times, spaces, rows, width), jnp.bfloat16),
            pltpu.VMEM((times * spaces, rows, 2 * width), jnp.bfloat16),
            pltpu.VMEM(w_qkv.shape, jnp.bfloat16),
            pltpu.VMEM(w_out.shape, jnp.bfloat16),
            pltpu.VMEM((2 * rows, width), jnp.bfloat16),
            pltpu.VMEM((capacity, width), jnp.bfloat16),
            pltpu.VMEM((capacity, width), jnp.float32),
            pltpu.SemaphoreType.DMA((3,)),
            pltpu.SemaphoreType.DMA((times,)),
            pltpu.SemaphoreType.DMA((times,)),
            pltpu.SemaphoreType.DMA((times,)),
            pltpu.SemaphoreType.DMA((times,)),
            pltpu.SemaphoreType.DMA((times,)),
        ],
        compiler_params=pltpu.CompilerParams(
            collective_id=0, has_side_effects=True, vmem_limit_bytes=VMEM_LIMIT
        ),
    )(
        activations.reshape(rows, width),
        attn_gain[None],
        attn_shift[None],
        w_qkv,
        b_qkv[None],
        w_out,
        b_out[None],
        final_gain[None],
        final_shift[None],
        mask_tokens.astype(jnp.float32),
        assignment.astype(jnp.float32)[None],
        jnp.asarray(columns),
    )


def solution(mesh):
    in_specs = (
        P(("clip", "tm"), "space", None),
        P(),
        P(),
        P(),
        P(),
        P(),
        P(),
        P(),
        P(),
        P("clip", None),
        P("clip"),
    )
    out_specs = P(("clip", "tm", "space"), None, None)
    return jax.shard_map(fused_local, mesh=mesh, in_specs=in_specs, out_specs=out_specs, check_vma=False)
```

```python
import functools
import math

import jax
import jax.numpy as jnp
import numpy as np
from jax import lax
from jax.experimental import pallas as pl
from jax.experimental.pallas import tpu as pltpu
from jax.sharding import PartitionSpec as P

HEADS = 16


EPSILON = 1e-06
FLOOR_SCORE = -1e30


def layer_norm(values, ln_gain, ln_shift):
    centre = jnp.mean(values, axis=-1, keepdims=True)
    deviation = values - centre
    variance = jnp.mean(deviation * deviation, axis=-1, keepdims=True)
    return deviation * lax.rsqrt(variance + EPSILON) * ln_gain + ln_shift


def start_state(query_heads):
    query_count, head_count, head_width = query_heads.shape
    return (
        jnp.full((head_count, query_count), FLOOR_SCORE, jnp.float32),
        jnp.zeros((head_count, query_count), jnp.float32),
        jnp.zeros((head_count, query_count, head_width), jnp.float32),
    )


def finish_state(carried_state):
    running_max, running_total, running_sum = carried_state
    return jnp.transpose(running_sum / running_total[:, :, None], (1, 0, 2)).astype(jnp.bfloat16)


def make_attend(query_heads):
    query_count, head_count, head_width = query_heads.shape
    score_scale = 1.0 / math.sqrt(head_width)

    def one_block(carried_state, kv_block):
        running_max, running_total, running_sum = carried_state
        block_length = kv_block.shape[1]
        key_rows = kv_block[0].reshape(block_length, head_count, head_width)
        value_rows = kv_block[1].reshape(block_length, head_count, head_width)
        scores = (
            jnp.einsum("qhe,khe->hqk", query_heads, key_rows, preferred_element_type=jnp.float32)
            * score_scale
        )
        new_max = jnp.maximum(running_max, jnp.max(scores, axis=-1))
        factor = jnp.exp(running_max - new_max)
        weights = jnp.exp(scores - new_max[:, :, None])
        running_total = running_total * factor + jnp.sum(weights, axis=-1)
        running_sum = running_sum * factor[:, :, None] + jnp.einsum(
            "hqk,khe->hqe",
            weights.astype(jnp.bfloat16),
            value_rows,
            preferred_element_type=jnp.float32,
        )
        return (new_max, running_total, running_sum)

    def attend(carried_state, key_piece, first_row):
        length = key_piece.shape[1]
        block_rows = length
        while block_rows > 1024 and block_rows % 2 == 0:
            block_rows = block_rows // 2

        def advance(position, carried):
            kv_block = lax.dynamic_slice_in_dim(key_piece, position * block_rows, block_rows, 1)
            return one_block(carried, kv_block)

        return lax.fori_loop(0, length // block_rows, advance, carried_state)

    return attend


def local(
    activations,
    attn_gain,
    attn_shift,
    w_qkv,
    b_qkv,
    w_out,
    b_out,
    final_gain,
    final_shift,
    mask_tokens,
    assignment,
):
    frame_count, patch_count, model_width = activations.shape
    local_rows = frame_count * patch_count
    head_width = model_width // HEADS
    tokens_flat = activations.reshape(local_rows, model_width)
    normed_in = layer_norm(tokens_flat.astype(jnp.float32), attn_gain, attn_shift).astype(
        jnp.bfloat16
    )
    projected = (jnp.dot(normed_in, w_qkv, preferred_element_type=jnp.float32) + b_qkv).astype(
        jnp.bfloat16
    )
    query_rows = projected[:, :model_width]
    paired = jnp.stack(
        (projected[:, model_width : 2 * model_width], projected[:, 2 * model_width :])
    )
    groups = lax.axis_size("space")
    group_heads = HEADS // groups
    stacked = jnp.stack((query_rows, paired[0], paired[1])).reshape(
        3, local_rows, groups, group_heads, head_width
    )
    swapped = lax.all_to_all(stacked, "space", split_axis=2, concat_axis=1, tiled=True)
    gathered_rows = swapped.shape[1]
    kept_heads = swapped.shape[3]
    query_heads = swapped[0].reshape(gathered_rows, kept_heads, head_width)
    kv_rows = swapped[1:].reshape(2, gathered_rows, kept_heads * head_width)
    time_state = make_attend(query_heads)(
        start_state(query_heads), lax.all_gather(kv_rows, "tm", axis=1, tiled=True), jnp.int32(0)
    )
    head_output = finish_state(time_state).reshape(gathered_rows, 1, kept_heads, head_width)
    merged = lax.all_to_all(head_output, "space", split_axis=0, concat_axis=1, tiled=True)
    attended = merged.reshape(local_rows, model_width)
    hidden = (
        tokens_flat.astype(jnp.float32)
        + jnp.dot(attended, w_out, preferred_element_type=jnp.float32)
        + b_out
    ).astype(jnp.bfloat16)
    normed = layer_norm(hidden.astype(jnp.float32), final_gain, final_shift).astype(jnp.bfloat16)
    owners = mask_tokens.shape[0]
    capacity = mask_tokens.shape[1]
    per_source = capacity // owners
    spaces = lax.axis_size("space")
    spatial = patch_count * spaces
    own_index = lax.axis_index("tm") * spaces + lax.axis_index("space")
    owner_lists = jnp.take(mask_tokens, assignment, axis=0)
    listed = owner_lists >= 0
    clipped = jnp.maximum(owner_lists, 0)
    token_frame = clipped // spatial
    token_patch = clipped % spatial
    home_device = token_frame // frame_count * spaces + token_patch // patch_count
    local_row = token_frame % frame_count * patch_count + token_patch % patch_count
    mine = listed & (home_device == own_index)
    slot_index = jnp.cumsum(mine.astype(jnp.int32), axis=1) - 1
    wanted = mine[:, None, :] & (
        slot_index[:, None, :] == jnp.arange(per_source, dtype=jnp.int32)[None, :, None]
    )
    picks = jnp.sum(jnp.where(wanted, local_row[:, None, :], 0), axis=-1)
    present = jnp.any(wanted, axis=-1)
    own_home = lax.dynamic_index_in_dim(home_device, own_index, 0, keepdims=False)
    own_listed = lax.dynamic_index_in_dim(listed, own_index, 0, keepdims=False)
    entry_order = jnp.arange(capacity, dtype=jnp.int32)
    earlier = (
        (entry_order[:, None] < entry_order[None, :])
        & own_listed[:, None]
        & (own_home[:, None] == own_home[None, :])
    )
    entry_rank = jnp.sum(earlier.astype(jnp.int32), axis=0)
    where_from = jnp.where(own_listed, own_home * per_source + entry_rank, 0)
    outgoing = jnp.where(
        present[:, :, None], jnp.take(normed, picks, axis=0), jnp.zeros((), jnp.bfloat16)
    )
    arrived = lax.all_to_all(outgoing, ("tm", "space"), split_axis=0, concat_axis=0, tiled=True)
    row_table = arrived.reshape(owners * per_source, model_width)
    placed = jnp.take(row_table, where_from, axis=0)
    return jnp.where(own_listed[:, None], placed, jnp.zeros((), jnp.bfloat16))[None]


LANES = 128
WINDOW = 256
VMEM_LIMIT = 60 * 1024 * 1024
MESH = pl.DeviceIdType.MESH


def norm_rows(values, gain, shift):
    return layer_norm(values.astype(jnp.float32), gain, shift).astype(jnp.bfloat16)


def fused_kernel(
    times,
    head_width,
    x_ref,
    gain_flat,
    shift_flat,
    w_qkv_ref,
    b_qkv_flat,
    w_out_ref,
    b_out_flat,
    final_gain_flat,
    final_shift_flat,
    lists_ref,
    assignment_ref,
    columns_ref,
    out_ref,
    x_all,
    kv_all,
    w_qkv,
    w_out,
    normed,
    queries,
    attended,
    b_qkv_ref,
    vectors,
    local_sem,
    up_send,
    down_send,
    side_send,
    line_recv,
    side_recv,
):
    me = lax.axis_index("tm")
    side = lax.axis_index("space")
    other = 1 - side
    rows, width = x_ref.shape
    load_x = pltpu.make_async_copy(x_ref, x_all.at[me, side], local_sem.at[0])
    load_qkv = pltpu.make_async_copy(w_qkv_ref, w_qkv, local_sem.at[1])
    load_out = pltpu.make_async_copy(w_out_ref, w_out, local_sem.at[2])
    load_x.start()
    load_qkv.start()
    load_out.start()

    has_up = me < times - 1
    has_down = me > 0

    barrier = pltpu.get_barrier_semaphore()
    pl.semaphore_signal(barrier, inc=1, device_id={"space": other}, device_id_type=MESH)

    @pl.when(has_up)
    def _():
        pl.semaphore_signal(barrier, inc=1, device_id={"tm": me + 1}, device_id_type=MESH)

    @pl.when(has_down)
    def _():
        pl.semaphore_signal(barrier, inc=1, device_id={"tm": me - 1}, device_id_type=MESH)

    pl.semaphore_wait(barrier, 1 + has_up.astype(jnp.int32) + has_down.astype(jnp.int32))

    def up_copy(source, block):
        return pltpu.make_async_remote_copy(
            source, x_all.at[block, side], up_send.at[block], line_recv.at[block],
            device_id={"tm": me + 1}, device_id_type=MESH,
        )

    def down_copy(source, block):
        return pltpu.make_async_remote_copy(
            source, x_all.at[block, side], down_send.at[block], line_recv.at[block],
            device_id={"tm": me - 1}, device_id_type=MESH,
        )

    def side_copy(source, block, from_side):
        return pltpu.make_async_remote_copy(
            source, x_all.at[block, from_side], side_send.at[block], side_recv.at[block],
            device_id={"space": other}, device_id_type=MESH,
        )

    @pl.when(has_up)
    def _():
        up_copy(x_ref, me).start()

    @pl.when(has_down)
    def _():
        down_copy(x_ref, me).start()

    side_copy(x_ref, me, side).start()

    b_qkv_ref[...] = b_qkv_flat[...].reshape(1, 3 * width)
    flats = (gain_flat, shift_flat, b_out_flat, final_gain_flat, final_shift_flat)
    for place, flat in enumerate(flats):
        vectors[place : place + 1, :] = flat[...].reshape(1, width)
    gain_ref, shift_ref, b_out_ref, final_gain_ref, final_shift_ref = (
        vectors.at[place : place + 1, :] for place in range(len(flats))
    )

    def arrive_and_forward(step):
        below, above = me - step, me + step

        @pl.when(below >= 0)
        def _():
            held = x_all.at[below, side]
            up_copy(held, below).wait_recv()

            @pl.when(has_up)
            def _():
                up_copy(held, below).start()

            side_copy(held, below, side).start()

        @pl.when(above < times)
        def _():
            held = x_all.at[above, side]
            down_copy(held, above).wait_recv()

            @pl.when(has_down)
            def _():
                down_copy(held, above).start()

            side_copy(held, above, side).start()

    reach = jnp.minimum(me, times - 1 - me)

    def ordered(place):
        if place == 0:
            return me
        near = me - (place + 1) // 2 if place % 2 else me + place // 2
        far_step = place - reach
        far = jnp.where(2 * me > times - 1, me - far_step, me + far_step)
        return jnp.where(place <= 2 * reach, near, far)

    tiles = 2 * width // WINDOW

    def project(blocks):
        count = len(blocks)
        for place, (block, from_side) in enumerate(blocks):
            normed[place * rows : (place + 1) * rows, :] = norm_rows(
                x_all[block, from_side], gain_ref[...], shift_ref[...]
            )

        def one_tile(tile, carried):
            start = pl.multiple_of(tile * WINDOW, WINDOW)
            shifted = pl.multiple_of(width + tile * WINDOW, LANES)
            made = jnp.dot(
                normed[: count * rows, :],
                w_qkv[:, pl.ds(shifted, WINDOW)],
                preferred_element_type=jnp.float32,
            )
            made = (made + b_qkv_ref[:, pl.ds(shifted, WINDOW)]).astype(jnp.bfloat16)
            for place, (block, from_side) in enumerate(blocks):
                kv_all[block * 2 + from_side, :, pl.ds(start, WINDOW)] = made[
                    place * rows : (place + 1) * rows, :
                ]
            return carried

        lax.fori_loop(0, tiles, one_tile, 0)

    load_x.wait()
    load_qkv.wait()
    project([(me, side)])
    for step in range(1, times):
        arrive_and_forward(step)
        earlier = ordered(step - 1)
        side_copy(x_all.at[earlier, other], earlier, other).wait_recv()
        project([(ordered(step), side), (earlier, other)])
    last = ordered(times - 1)
    side_copy(x_all.at[last, other], last, other).wait_recv()
    project([(last, other)])

    owner = assignment_ref[me * 2 + side]
    list_places = lax.broadcasted_iota(jnp.int32, lists_ref.shape, 0)
    lists = lists_ref[...].astype(jnp.float32)
    token_row = jnp.sum(jnp.where(list_places == owner, lists, 0.0), axis=0, keepdims=True)
    capacity = lists_ref.shape[1]
    diagonal = lax.broadcasted_iota(jnp.int32, (capacity, capacity), 0) == lax.broadcasted_iota(
        jnp.int32, (capacity, capacity), 1
    )
    tokens = jnp.sum(jnp.where(diagonal, token_row, 0.0), axis=1, keepdims=True)
    one_hot = (tokens == columns_ref[...]).astype(jnp.float32).astype(jnp.bfloat16)
    picked = jnp.dot(
        one_hot,
        x_all[...].reshape(times * 2 * rows, width),
        preferred_element_type=jnp.float32,
    )
    out_ref[0] = picked.astype(jnp.bfloat16)
    queries[...] = (
        jnp.dot(
            norm_rows(picked, gain_ref[...], shift_ref[...]),
            w_qkv[:, :width],
            preferred_element_type=jnp.float32,
        )
        + b_qkv_ref[:, :width]
    ).astype(jnp.bfloat16)
    attended[...] = jnp.zeros_like(attended)
    score_scale = math.log2(math.e) / math.sqrt(head_width)
    all_rows = times * 2 * rows

    def one_head(head, carried):
        first = head * head_width
        base = pl.multiple_of(jnp.minimum(first // LANES, width // LANES - 2) * LANES, LANES)
        value_base = pl.multiple_of(base + width, LANES)
        lane = lax.broadcasted_iota(jnp.int32, (capacity, WINDOW), 1) + base
        inside = (lane >= first) & (lane < first + head_width)
        query = jnp.where(inside, queries[:, pl.ds(base, WINDOW)].astype(jnp.float32), 0.0)
        keys = kv_all[:, :, pl.ds(base, WINDOW)].reshape(all_rows, WINDOW)
        values = kv_all[:, :, pl.ds(value_base, WINDOW)].reshape(all_rows, WINDOW)
        scores = (
            lax.dot_general(
                query.astype(jnp.bfloat16), keys, (((1,), (1,)), ((), ())),
                preferred_element_type=jnp.float32,
            )
            * score_scale
        )
        weights = jnp.exp2(scores - jnp.max(scores, axis=1, keepdims=True))
        totals = jnp.sum(weights, axis=1, keepdims=True)
        summed = jnp.dot(weights.astype(jnp.bfloat16), values, preferred_element_type=jnp.float32)
        attended[:, pl.ds(base, WINDOW)] += jnp.where(inside, summed / totals, 0.0)
        return carried

    lax.fori_loop(0, HEADS, one_head, 0)
    load_out.wait()
    hidden = (
        out_ref[0].astype(jnp.float32)
        + jnp.dot(
            attended[...].astype(jnp.bfloat16), w_out[...], preferred_element_type=jnp.float32
        )
        + b_out_ref[...]
    ).astype(jnp.bfloat16)
    final = layer_norm(hidden.astype(jnp.float32), final_gain_ref[...], final_shift_ref[...])
    out_ref[0] = jnp.where(tokens >= 0, final, 0.0).astype(jnp.bfloat16)

    for block in range(times):

        @pl.when(has_up & (block <= me))
        def _():
            up_copy(x_all.at[block, side], block).wait_send()

        @pl.when(has_down & (block >= me))
        def _():
            down_copy(x_all.at[block, side], block).wait_send()

        side_copy(x_all.at[block, side], block, side).wait_send()


def fits_fused(times, spaces, rows, width, capacity):
    all_rows = times * spaces * rows
    held = 2 * (all_rows * width * 3 + width * width * 4 + 2 * rows * width)
    held += 4 * capacity * (width * 2 + all_rows * 3)
    return (
        spaces == 2
        and held < VMEM_LIMIT
        and width % LANES == 0
        and width // HEADS <= LANES
        and rows % 16 == 0
    )


def fused_local(
    activations,
    attn_gain,
    attn_shift,
    w_qkv,
    b_qkv,
    w_out,
    b_out,
    final_gain,
    final_shift,
    mask_tokens,
    assignment,
):
    frames, patches, width = activations.shape
    rows = frames * patches
    times = lax.axis_size("tm")
    spaces = lax.axis_size("space")
    if not fits_fused(times, spaces, rows, width, mask_tokens.shape[1]):
        return local(
            activations, attn_gain, attn_shift, w_qkv, b_qkv, w_out, b_out,
            final_gain, final_shift, mask_tokens, assignment,
        )
    capacity = mask_tokens.shape[1]
    order = np.arange(times * frames * spaces * patches).reshape(times, frames, spaces, patches)
    columns = order.transpose(0, 2, 1, 3).reshape(1, -1).astype(np.float32)
    vmem = pl.BlockSpec(memory_space=pltpu.VMEM)
    hbm = pl.BlockSpec(memory_space=pl.ANY)
    smem = pl.BlockSpec(memory_space=pltpu.SMEM)
    return pl.pallas_call(
        functools.partial(fused_kernel, times, width // HEADS),
        out_shape=jax.ShapeDtypeStruct((1, capacity, width), jnp.bfloat16),
        in_specs=[vmem, vmem, vmem, hbm, vmem, hbm, vmem, vmem, vmem, vmem, smem, vmem],
        out_specs=vmem,
        scratch_shapes=[
            pltpu.VMEM((times, spaces, rows, width), jnp.bfloat16),
            pltpu.VMEM((times * spaces, rows, 2 * width), jnp.bfloat16),
            pltpu.VMEM(w_qkv.shape, jnp.bfloat16),
            pltpu.VMEM(w_out.shape, jnp.bfloat16),
            pltpu.VMEM((2 * rows, width), jnp.bfloat16),
            pltpu.VMEM((capacity, width), jnp.bfloat16),
            pltpu.VMEM((capacity, width), jnp.float32),
            pltpu.VMEM((1, 3 * width), jnp.float32),
            pltpu.VMEM((5, width), jnp.float32),
            pltpu.SemaphoreType.DMA((3,)),
            pltpu.SemaphoreType.DMA((times,)),
            pltpu.SemaphoreType.DMA((times,)),
            pltpu.SemaphoreType.DMA((times,)),
            pltpu.SemaphoreType.DMA((times,)),
            pltpu.SemaphoreType.DMA((times,)),
        ],
        compiler_params=pltpu.CompilerParams(
            collective_id=0, has_side_effects=True, vmem_limit_bytes=VMEM_LIMIT
        ),
    )(
        activations.reshape(rows, width),
        attn_gain,
        attn_shift,
        w_qkv,
        b_qkv,
        w_out,
        b_out,
        final_gain,
        final_shift,
        mask_tokens,
        assignment,
        jnp.asarray(columns),
    )


def solution(mesh):
    in_specs = (
        P(("clip", "tm"), "space", None),
        P(),
        P(),
        P(),
        P(),
        P(),
        P(),
        P(),
        P(),
        P("clip", None),
        P("clip"),
    )
    out_specs = P(("clip", "tm", "space"), None, None)
    return jax.shard_map(fused_local, mesh=mesh, in_specs=in_specs, out_specs=out_specs, check_vma=False)
```

```python
import functools
import math

import jax
import jax.numpy as jnp
import numpy as np
from jax import lax
from jax.experimental import pallas as pl
from jax.experimental.pallas import tpu as pltpu
from jax.sharding import PartitionSpec as P

HEADS = 16


EPSILON = 1e-06
FLOOR_SCORE = -1e30


def layer_norm(values, ln_gain, ln_shift):
    centre = jnp.mean(values, axis=-1, keepdims=True)
    deviation = values - centre
    variance = jnp.mean(deviation * deviation, axis=-1, keepdims=True)
    return deviation * lax.rsqrt(variance + EPSILON) * ln_gain + ln_shift


def start_state(query_heads):
    query_count, head_count, head_width = query_heads.shape
    return (
        jnp.full((head_count, query_count), FLOOR_SCORE, jnp.float32),
        jnp.zeros((head_count, query_count), jnp.float32),
        jnp.zeros((head_count, query_count, head_width), jnp.float32),
    )


def finish_state(carried_state):
    running_max, running_total, running_sum = carried_state
    return jnp.transpose(running_sum / running_total[:, :, None], (1, 0, 2)).astype(jnp.bfloat16)


def make_attend(query_heads):
    query_count, head_count, head_width = query_heads.shape
    score_scale = 1.0 / math.sqrt(head_width)

    def one_block(carried_state, kv_block):
        running_max, running_total, running_sum = carried_state
        block_length = kv_block.shape[1]
        key_rows = kv_block[0].reshape(block_length, head_count, head_width)
        value_rows = kv_block[1].reshape(block_length, head_count, head_width)
        scores = (
            jnp.einsum("qhe,khe->hqk", query_heads, key_rows, preferred_element_type=jnp.float32)
            * score_scale
        )
        new_max = jnp.maximum(running_max, jnp.max(scores, axis=-1))
        factor = jnp.exp(running_max - new_max)
        weights = jnp.exp(scores - new_max[:, :, None])
        running_total = running_total * factor + jnp.sum(weights, axis=-1)
        running_sum = running_sum * factor[:, :, None] + jnp.einsum(
            "hqk,khe->hqe",
            weights.astype(jnp.bfloat16),
            value_rows,
            preferred_element_type=jnp.float32,
        )
        return (new_max, running_total, running_sum)

    def attend(carried_state, key_piece, first_row):
        length = key_piece.shape[1]
        block_rows = length
        while block_rows > 1024 and block_rows % 2 == 0:
            block_rows = block_rows // 2

        def advance(position, carried):
            kv_block = lax.dynamic_slice_in_dim(key_piece, position * block_rows, block_rows, 1)
            return one_block(carried, kv_block)

        return lax.fori_loop(0, length // block_rows, advance, carried_state)

    return attend


def local(
    activations,
    attn_gain,
    attn_shift,
    w_qkv,
    b_qkv,
    w_out,
    b_out,
    final_gain,
    final_shift,
    mask_tokens,
    assignment,
):
    frame_count, patch_count, model_width = activations.shape
    local_rows = frame_count * patch_count
    head_width = model_width // HEADS
    tokens_flat = activations.reshape(local_rows, model_width)
    normed_in = layer_norm(tokens_flat.astype(jnp.float32), attn_gain, attn_shift).astype(
        jnp.bfloat16
    )
    projected = (jnp.dot(normed_in, w_qkv, preferred_element_type=jnp.float32) + b_qkv).astype(
        jnp.bfloat16
    )
    query_rows = projected[:, :model_width]
    paired = jnp.stack(
        (projected[:, model_width : 2 * model_width], projected[:, 2 * model_width :])
    )
    groups = lax.axis_size("space")
    group_heads = HEADS // groups
    stacked = jnp.stack((query_rows, paired[0], paired[1])).reshape(
        3, local_rows, groups, group_heads, head_width
    )
    swapped = lax.all_to_all(stacked, "space", split_axis=2, concat_axis=1, tiled=True)
    gathered_rows = swapped.shape[1]
    kept_heads = swapped.shape[3]
    query_heads = swapped[0].reshape(gathered_rows, kept_heads, head_width)
    kv_rows = swapped[1:].reshape(2, gathered_rows, kept_heads * head_width)
    time_state = make_attend(query_heads)(
        start_state(query_heads), lax.all_gather(kv_rows, "tm", axis=1, tiled=True), jnp.int32(0)
    )
    head_output = finish_state(time_state).reshape(gathered_rows, 1, kept_heads, head_width)
    merged = lax.all_to_all(head_output, "space", split_axis=0, concat_axis=1, tiled=True)
    attended = merged.reshape(local_rows, model_width)
    hidden = (
        tokens_flat.astype(jnp.float32)
        + jnp.dot(attended, w_out, preferred_element_type=jnp.float32)
        + b_out
    ).astype(jnp.bfloat16)
    normed = layer_norm(hidden.astype(jnp.float32), final_gain, final_shift).astype(jnp.bfloat16)
    owners = mask_tokens.shape[0]
    capacity = mask_tokens.shape[1]
    per_source = capacity // owners
    spaces = lax.axis_size("space")
    spatial = patch_count * spaces
    own_index = lax.axis_index("tm") * spaces + lax.axis_index("space")
    owner_lists = jnp.take(mask_tokens, assignment, axis=0)
    listed = owner_lists >= 0
    clipped = jnp.maximum(owner_lists, 0)
    token_frame = clipped // spatial
    token_patch = clipped % spatial
    home_device = token_frame // frame_count * spaces + token_patch // patch_count
    local_row = token_frame % frame_count * patch_count + token_patch % patch_count
    mine = listed & (home_device == own_index)
    slot_index = jnp.cumsum(mine.astype(jnp.int32), axis=1) - 1
    wanted = mine[:, None, :] & (
        slot_index[:, None, :] == jnp.arange(per_source, dtype=jnp.int32)[None, :, None]
    )
    picks = jnp.sum(jnp.where(wanted, local_row[:, None, :], 0), axis=-1)
    present = jnp.any(wanted, axis=-1)
    own_home = lax.dynamic_index_in_dim(home_device, own_index, 0, keepdims=False)
    own_listed = lax.dynamic_index_in_dim(listed, own_index, 0, keepdims=False)
    entry_order = jnp.arange(capacity, dtype=jnp.int32)
    earlier = (
        (entry_order[:, None] < entry_order[None, :])
        & own_listed[:, None]
        & (own_home[:, None] == own_home[None, :])
    )
    entry_rank = jnp.sum(earlier.astype(jnp.int32), axis=0)
    where_from = jnp.where(own_listed, own_home * per_source + entry_rank, 0)
    outgoing = jnp.where(
        present[:, :, None], jnp.take(normed, picks, axis=0), jnp.zeros((), jnp.bfloat16)
    )
    arrived = lax.all_to_all(outgoing, ("tm", "space"), split_axis=0, concat_axis=0, tiled=True)
    row_table = arrived.reshape(owners * per_source, model_width)
    placed = jnp.take(row_table, where_from, axis=0)
    return jnp.where(own_listed[:, None], placed, jnp.zeros((), jnp.bfloat16))[None]


LANES = 128
WINDOW = 256
VMEM_LIMIT = 60 * 1024 * 1024
MESH = pl.DeviceIdType.MESH


def norm_rows(values, gain, shift):
    return layer_norm(values.astype(jnp.float32), gain, shift).astype(jnp.bfloat16)


def fused_kernel(
    times,
    head_width,
    x_ref,
    gain_flat,
    shift_flat,
    w_qkv_ref,
    b_qkv_flat,
    w_out_ref,
    b_out_flat,
    final_gain_flat,
    final_shift_flat,
    lists_ref,
    assignment_ref,
    columns_ref,
    out_ref,
    x_all,
    kv_all,
    w_qkv,
    w_out,
    normed,
    queries,
    attended,
    b_qkv_ref,
    vectors,
    local_sem,
    up_send,
    down_send,
    side_send,
    line_recv,
    side_recv,
    mate_sem,
):
    me = lax.axis_index("tm")
    side = lax.axis_index("space")
    other = 1 - side
    rows, width = x_ref.shape
    half_rows = rows // 2
    mate = me + 1 - 2 * lax.rem(me, 2)
    load_x = [
        pltpu.make_async_copy(
            x_ref.at[pl.ds(half * half_rows, half_rows)],
            x_all.at[me, side, half],
            local_sem.at[2 + half],
        )
        for half in range(2)
    ]
    load_qkv = pltpu.make_async_copy(w_qkv_ref, w_qkv, local_sem.at[0])
    load_out = pltpu.make_async_copy(w_out_ref, w_out, local_sem.at[1])
    for load in load_x:
        load.start()
    load_qkv.start()
    load_out.start()

    has_up = me < times - 1
    has_down = me > 0

    barrier = pltpu.get_barrier_semaphore()
    pl.semaphore_signal(barrier, inc=1, device_id={"space": other}, device_id_type=MESH)

    @pl.when(has_up)
    def _():
        pl.semaphore_signal(barrier, inc=1, device_id={"tm": me + 1}, device_id_type=MESH)

    @pl.when(has_down)
    def _():
        pl.semaphore_signal(barrier, inc=1, device_id={"tm": me - 1}, device_id_type=MESH)

    pl.semaphore_wait(barrier, 1 + has_up.astype(jnp.int32) + has_down.astype(jnp.int32))

    def up_copy(source, block, half):
        return pltpu.make_async_remote_copy(
            source, x_all.at[block, side, half], up_send.at[block, half],
            line_recv.at[block, half], device_id={"tm": me + 1}, device_id_type=MESH,
        )

    def down_copy(source, block, half):
        return pltpu.make_async_remote_copy(
            source, x_all.at[block, side, half], down_send.at[block, half],
            line_recv.at[block, half], device_id={"tm": me - 1}, device_id_type=MESH,
        )

    def side_copy(block, half, from_side, source=None):
        place = x_all.at[block, from_side, half]
        return pltpu.make_async_remote_copy(
            place if source is None else source, place, side_send.at[block, half],
            side_recv.at[block, half], device_id={"space": other}, device_id_type=MESH,
        )

    def mate_copy(block):
        place = x_all.at[block, other, 1]
        return pltpu.make_async_remote_copy(
            place, place, mate_sem.at[0], mate_sem.at[1],
            device_id={"tm": mate}, device_id_type=MESH,
        )

    for half in range(2):
        own_half = x_ref.at[pl.ds(half * half_rows, half_rows)]

        @pl.when(has_up)
        def _():
            up_copy(own_half, me, half).start()

        @pl.when(has_down)
        def _():
            down_copy(own_half, me, half).start()

        side_copy(me, half, side, own_half).start()

    b_qkv_ref[...] = b_qkv_flat[...].reshape(1, 3 * width)
    flats = (gain_flat, shift_flat, b_out_flat, final_gain_flat, final_shift_flat)
    for place, flat in enumerate(flats):
        vectors[place : place + 1, :] = flat[...].reshape(1, width)
    gain_ref, shift_ref, b_out_ref, final_gain_ref, final_shift_ref = (
        vectors.at[place : place + 1, :] for place in range(len(flats))
    )

    def send_aside(block, half):
        if half == 0:
            side_copy(block, half, side).start()
        else:

            @pl.when(block != mate)
            def _():
                side_copy(block, half, side).start()

    def arrive_and_forward(step, half):
        below, above = me - step, me + step

        @pl.when(below >= 0)
        def _():
            held = x_all.at[below, side, half]
            up_copy(held, below, half).wait_recv()

            @pl.when(has_up)
            def _():
                up_copy(held, below, half).start()

            send_aside(below, half)

        @pl.when(above < times)
        def _():
            held = x_all.at[above, side, half]
            down_copy(held, above, half).wait_recv()

            @pl.when(has_down)
            def _():
                down_copy(held, above, half).start()

            send_aside(above, half)

    reach = jnp.minimum(me, times - 1 - me)
    toward = mate - me

    def ordered(place):
        if place == 0:
            return me
        near = me + ((place + 1) // 2) * (toward if place % 2 else -toward)
        far_step = place - reach
        far = jnp.where(2 * me > times - 1, me - far_step, me + far_step)
        return jnp.where(place <= 2 * reach, near, far)

    tiles = 2 * width // WINDOW

    def project(pieces):
        count = len(pieces)
        for place, (block, from_side, half) in enumerate(pieces):
            normed[place * half_rows : (place + 1) * half_rows, :] = norm_rows(
                x_all[block, from_side, half], gain_ref[...], shift_ref[...]
            )

        def one_tile(tile, carried):
            start = pl.multiple_of(tile * WINDOW, WINDOW)
            shifted = pl.multiple_of(width + tile * WINDOW, LANES)
            made = jnp.dot(
                normed[: count * half_rows, :],
                w_qkv[:, pl.ds(shifted, WINDOW)],
                preferred_element_type=jnp.float32,
            )
            made = (made + b_qkv_ref[:, pl.ds(shifted, WINDOW)]).astype(jnp.bfloat16)
            for place, (block, from_side, half) in enumerate(pieces):
                kv_all[block * 2 + from_side, half, :, pl.ds(start, WINDOW)] = made[
                    place * half_rows : (place + 1) * half_rows, :
                ]
            return carried

        lax.fori_loop(0, tiles, one_tile, 0)

    def from_aside(place):
        block = ordered(place)
        pieces = []
        for half in range(1 if place == 1 else 2):
            side_copy(block, half, other).wait_recv()
            pieces.append((block, other, half))
        return pieces

    for load in load_x:
        load.wait()
    load_qkv.wait()
    project([(me, side, 0), (me, side, 1)])
    last = ordered(times - 1)
    for step in range(1, times - 1):
        arrive_and_forward(step, 0)
        arrive_and_forward(step, 1)
        ready = from_aside(step - 1)
        if step == times - 2:
            mate_copy(me).start()
        project([(ordered(step), side, 0), (ordered(step), side, 1)] + ready)
    arrive_and_forward(times - 1, 0)
    project([(last, side, 0)] + from_aside(times - 2))
    arrive_and_forward(times - 1, 1)
    side_copy(last, 0, other).wait_recv()
    project([(last, side, 1), (last, other, 0)])
    side_copy(last, 1, other).wait_recv()
    mate_copy(mate).wait_recv()
    project([(last, other, 1), (mate, other, 1)])

    owner = assignment_ref[me * 2 + side]
    list_places = lax.broadcasted_iota(jnp.int32, lists_ref.shape, 0)
    lists = lists_ref[...].astype(jnp.float32)
    token_row = jnp.sum(jnp.where(list_places == owner, lists, 0.0), axis=0, keepdims=True)
    capacity = lists_ref.shape[1]
    diagonal = lax.broadcasted_iota(jnp.int32, (capacity, capacity), 0) == lax.broadcasted_iota(
        jnp.int32, (capacity, capacity), 1
    )
    tokens = jnp.sum(jnp.where(diagonal, token_row, 0.0), axis=1, keepdims=True)
    one_hot = (tokens == columns_ref[...]).astype(jnp.float32).astype(jnp.bfloat16)
    picked = jnp.dot(
        one_hot,
        x_all[...].reshape(times * 2 * rows, width),
        preferred_element_type=jnp.float32,
    )
    out_ref[0] = picked.astype(jnp.bfloat16)
    queries[...] = (
        jnp.dot(
            norm_rows(picked, gain_ref[...], shift_ref[...]),
            w_qkv[:, :width],
            preferred_element_type=jnp.float32,
        )
        + b_qkv_ref[:, :width]
    ).astype(jnp.bfloat16)
    attended[...] = jnp.zeros_like(attended)
    score_scale = math.log2(math.e) / math.sqrt(head_width)
    all_rows = times * 2 * rows

    def one_head(head, carried):
        first = head * head_width
        base = pl.multiple_of(jnp.minimum(first // LANES, width // LANES - 2) * LANES, LANES)
        value_base = pl.multiple_of(base + width, LANES)
        lane = lax.broadcasted_iota(jnp.int32, (capacity, WINDOW), 1) + base
        inside = (lane >= first) & (lane < first + head_width)
        query = jnp.where(inside, queries[:, pl.ds(base, WINDOW)].astype(jnp.float32), 0.0)
        keys = kv_all[:, :, :, pl.ds(base, WINDOW)].reshape(all_rows, WINDOW)
        values = kv_all[:, :, :, pl.ds(value_base, WINDOW)].reshape(all_rows, WINDOW)
        scores = (
            lax.dot_general(
                query.astype(jnp.bfloat16), keys, (((1,), (1,)), ((), ())),
                preferred_element_type=jnp.float32,
            )
            * score_scale
        )
        weights = jnp.exp2(scores - jnp.max(scores, axis=1, keepdims=True))
        totals = jnp.sum(weights, axis=1, keepdims=True)
        summed = jnp.dot(weights.astype(jnp.bfloat16), values, preferred_element_type=jnp.float32)
        attended[:, pl.ds(base, WINDOW)] += jnp.where(inside, summed / totals, 0.0)
        return carried

    lax.fori_loop(0, HEADS, one_head, 0, unroll=4)
    load_out.wait()
    hidden = (
        out_ref[0].astype(jnp.float32)
        + jnp.dot(
            attended[...].astype(jnp.bfloat16), w_out[...], preferred_element_type=jnp.float32
        )
        + b_out_ref[...]
    ).astype(jnp.bfloat16)
    final = layer_norm(hidden.astype(jnp.float32), final_gain_ref[...], final_shift_ref[...])
    out_ref[0] = jnp.where(tokens >= 0, final, 0.0).astype(jnp.bfloat16)

    for block in range(times):
        for half in range(2):

            @pl.when(has_up & (block <= me))
            def _():
                up_copy(x_all.at[block, side, half], block, half).wait_send()

            @pl.when(has_down & (block >= me))
            def _():
                down_copy(x_all.at[block, side, half], block, half).wait_send()

            @pl.when((block != mate) | (half == 0))
            def _():
                side_copy(block, half, side).wait_send()

    mate_copy(me).wait_send()


def fits_fused(times, spaces, rows, width, capacity):
    all_rows = times * spaces * rows
    held = 2 * (all_rows * width * 3 + width * width * 4 + 2 * rows * width)
    held += 4 * capacity * (width * 2 + all_rows * 3)
    return (
        spaces == 2
        and held < VMEM_LIMIT
        and width % LANES == 0
        and width // HEADS <= LANES
        and rows % 32 == 0
        and times % 2 == 0
        and times > 2
    )


def fused_local(
    activations,
    attn_gain,
    attn_shift,
    w_qkv,
    b_qkv,
    w_out,
    b_out,
    final_gain,
    final_shift,
    mask_tokens,
    assignment,
):
    frames, patches, width = activations.shape
    rows = frames * patches
    times = lax.axis_size("tm")
    spaces = lax.axis_size("space")
    if not fits_fused(times, spaces, rows, width, mask_tokens.shape[1]):
        return local(
            activations, attn_gain, attn_shift, w_qkv, b_qkv, w_out, b_out,
            final_gain, final_shift, mask_tokens, assignment,
        )
    capacity = mask_tokens.shape[1]
    order = np.arange(times * frames * spaces * patches).reshape(times, frames, spaces, patches)
    columns = order.transpose(0, 2, 1, 3).reshape(1, -1).astype(np.float32)
    vmem = pl.BlockSpec(memory_space=pltpu.VMEM)
    hbm = pl.BlockSpec(memory_space=pl.ANY)
    smem = pl.BlockSpec(memory_space=pltpu.SMEM)
    return pl.pallas_call(
        functools.partial(fused_kernel, times, width // HEADS),
        out_shape=jax.ShapeDtypeStruct((1, capacity, width), jnp.bfloat16),
        in_specs=[vmem, vmem, vmem, hbm, vmem, hbm, vmem, vmem, vmem, vmem, smem, vmem],
        out_specs=vmem,
        scratch_shapes=[
            pltpu.VMEM((times, spaces, 2, rows // 2, width), jnp.bfloat16),
            pltpu.VMEM((times * spaces, 2, rows // 2, 2 * width), jnp.bfloat16),
            pltpu.VMEM(w_qkv.shape, jnp.bfloat16),
            pltpu.VMEM(w_out.shape, jnp.bfloat16),
            pltpu.VMEM((2 * rows, width), jnp.bfloat16),
            pltpu.VMEM((capacity, width), jnp.bfloat16),
            pltpu.VMEM((capacity, width), jnp.float32),
            pltpu.VMEM((1, 3 * width), jnp.float32),
            pltpu.VMEM((5, width), jnp.float32),
            pltpu.SemaphoreType.DMA((4,)),
            pltpu.SemaphoreType.DMA((times, 2)),
            pltpu.SemaphoreType.DMA((times, 2)),
            pltpu.SemaphoreType.DMA((times, 2)),
            pltpu.SemaphoreType.DMA((times, 2)),
            pltpu.SemaphoreType.DMA((times, 2)),
            pltpu.SemaphoreType.DMA((2,)),
        ],
        compiler_params=pltpu.CompilerParams(
            collective_id=0, has_side_effects=True, vmem_limit_bytes=VMEM_LIMIT
        ),
    )(
        activations.reshape(rows, width),
        attn_gain,
        attn_shift,
        w_qkv,
        b_qkv,
        w_out,
        b_out,
        final_gain,
        final_shift,
        mask_tokens,
        assignment,
        jnp.asarray(columns),
    )


def solution(mesh):
    in_specs = (
        P(("clip", "tm"), "space", None),
        P(),
        P(),
        P(),
        P(),
        P(),
        P(),
        P(),
        P(),
        P("clip", None),
        P("clip"),
    )
    out_specs = P(("clip", "tm", "space"), None, None)
    return jax.shard_map(fused_local, mesh=mesh, in_specs=in_specs, out_specs=out_specs, check_vma=False)
```

```python
import functools
import math

import jax
import jax.numpy as jnp
import numpy as np
from jax import lax
from jax.experimental import pallas as pl
from jax.experimental.pallas import tpu as pltpu
from jax.sharding import PartitionSpec as P

HEADS = 16


EPSILON = 1e-06
FLOOR_SCORE = -1e30


def layer_norm(values, ln_gain, ln_shift):
    centre = jnp.mean(values, axis=-1, keepdims=True)
    deviation = values - centre
    variance = jnp.mean(deviation * deviation, axis=-1, keepdims=True)
    return deviation * lax.rsqrt(variance + EPSILON) * ln_gain + ln_shift


def start_state(query_heads):
    query_count, head_count, head_width = query_heads.shape
    return (
        jnp.full((head_count, query_count), FLOOR_SCORE, jnp.float32),
        jnp.zeros((head_count, query_count), jnp.float32),
        jnp.zeros((head_count, query_count, head_width), jnp.float32),
    )


def finish_state(carried_state):
    running_max, running_total, running_sum = carried_state
    return jnp.transpose(running_sum / running_total[:, :, None], (1, 0, 2)).astype(jnp.bfloat16)


def make_attend(query_heads):
    query_count, head_count, head_width = query_heads.shape
    score_scale = 1.0 / math.sqrt(head_width)

    def one_block(carried_state, kv_block):
        running_max, running_total, running_sum = carried_state
        block_length = kv_block.shape[1]
        key_rows = kv_block[0].reshape(block_length, head_count, head_width)
        value_rows = kv_block[1].reshape(block_length, head_count, head_width)
        scores = (
            jnp.einsum("qhe,khe->hqk", query_heads, key_rows, preferred_element_type=jnp.float32)
            * score_scale
        )
        new_max = jnp.maximum(running_max, jnp.max(scores, axis=-1))
        factor = jnp.exp(running_max - new_max)
        weights = jnp.exp(scores - new_max[:, :, None])
        running_total = running_total * factor + jnp.sum(weights, axis=-1)
        running_sum = running_sum * factor[:, :, None] + jnp.einsum(
            "hqk,khe->hqe",
            weights.astype(jnp.bfloat16),
            value_rows,
            preferred_element_type=jnp.float32,
        )
        return (new_max, running_total, running_sum)

    def attend(carried_state, key_piece, first_row):
        length = key_piece.shape[1]
        block_rows = length
        while block_rows > 1024 and block_rows % 2 == 0:
            block_rows = block_rows // 2

        def advance(position, carried):
            kv_block = lax.dynamic_slice_in_dim(key_piece, position * block_rows, block_rows, 1)
            return one_block(carried, kv_block)

        return lax.fori_loop(0, length // block_rows, advance, carried_state)

    return attend


def local(
    activations,
    attn_gain,
    attn_shift,
    w_qkv,
    b_qkv,
    w_out,
    b_out,
    final_gain,
    final_shift,
    mask_tokens,
    assignment,
):
    frame_count, patch_count, model_width = activations.shape
    local_rows = frame_count * patch_count
    head_width = model_width // HEADS
    tokens_flat = activations.reshape(local_rows, model_width)
    normed_in = layer_norm(tokens_flat.astype(jnp.float32), attn_gain, attn_shift).astype(
        jnp.bfloat16
    )
    projected = (jnp.dot(normed_in, w_qkv, preferred_element_type=jnp.float32) + b_qkv).astype(
        jnp.bfloat16
    )
    query_rows = projected[:, :model_width]
    paired = jnp.stack(
        (projected[:, model_width : 2 * model_width], projected[:, 2 * model_width :])
    )
    groups = lax.axis_size("space")
    group_heads = HEADS // groups
    stacked = jnp.stack((query_rows, paired[0], paired[1])).reshape(
        3, local_rows, groups, group_heads, head_width
    )
    swapped = lax.all_to_all(stacked, "space", split_axis=2, concat_axis=1, tiled=True)
    gathered_rows = swapped.shape[1]
    kept_heads = swapped.shape[3]
    query_heads = swapped[0].reshape(gathered_rows, kept_heads, head_width)
    kv_rows = swapped[1:].reshape(2, gathered_rows, kept_heads * head_width)
    time_state = make_attend(query_heads)(
        start_state(query_heads), lax.all_gather(kv_rows, "tm", axis=1, tiled=True), jnp.int32(0)
    )
    head_output = finish_state(time_state).reshape(gathered_rows, 1, kept_heads, head_width)
    merged = lax.all_to_all(head_output, "space", split_axis=0, concat_axis=1, tiled=True)
    attended = merged.reshape(local_rows, model_width)
    hidden = (
        tokens_flat.astype(jnp.float32)
        + jnp.dot(attended, w_out, preferred_element_type=jnp.float32)
        + b_out
    ).astype(jnp.bfloat16)
    normed = layer_norm(hidden.astype(jnp.float32), final_gain, final_shift).astype(jnp.bfloat16)
    owners = mask_tokens.shape[0]
    capacity = mask_tokens.shape[1]
    per_source = capacity // owners
    spaces = lax.axis_size("space")
    spatial = patch_count * spaces
    own_index = lax.axis_index("tm") * spaces + lax.axis_index("space")
    owner_lists = jnp.take(mask_tokens, assignment, axis=0)
    listed = owner_lists >= 0
    clipped = jnp.maximum(owner_lists, 0)
    token_frame = clipped // spatial
    token_patch = clipped % spatial
    home_device = token_frame // frame_count * spaces + token_patch // patch_count
    local_row = token_frame % frame_count * patch_count + token_patch % patch_count
    mine = listed & (home_device == own_index)
    slot_index = jnp.cumsum(mine.astype(jnp.int32), axis=1) - 1
    wanted = mine[:, None, :] & (
        slot_index[:, None, :] == jnp.arange(per_source, dtype=jnp.int32)[None, :, None]
    )
    picks = jnp.sum(jnp.where(wanted, local_row[:, None, :], 0), axis=-1)
    present = jnp.any(wanted, axis=-1)
    own_home = lax.dynamic_index_in_dim(home_device, own_index, 0, keepdims=False)
    own_listed = lax.dynamic_index_in_dim(listed, own_index, 0, keepdims=False)
    entry_order = jnp.arange(capacity, dtype=jnp.int32)
    earlier = (
        (entry_order[:, None] < entry_order[None, :])
        & own_listed[:, None]
        & (own_home[:, None] == own_home[None, :])
    )
    entry_rank = jnp.sum(earlier.astype(jnp.int32), axis=0)
    where_from = jnp.where(own_listed, own_home * per_source + entry_rank, 0)
    outgoing = jnp.where(
        present[:, :, None], jnp.take(normed, picks, axis=0), jnp.zeros((), jnp.bfloat16)
    )
    arrived = lax.all_to_all(outgoing, ("tm", "space"), split_axis=0, concat_axis=0, tiled=True)
    row_table = arrived.reshape(owners * per_source, model_width)
    placed = jnp.take(row_table, where_from, axis=0)
    return jnp.where(own_listed[:, None], placed, jnp.zeros((), jnp.bfloat16))[None]


LANES = 128
WINDOW = 256
VMEM_LIMIT = 60 * 1024 * 1024
MESH = pl.DeviceIdType.MESH


def norm_rows(values, gain, shift):
    return layer_norm(values.astype(jnp.float32), gain, shift).astype(jnp.bfloat16)


def fused_kernel(
    times,
    head_width,
    x_ref,
    gain_flat,
    shift_flat,
    w_qkv_ref,
    b_qkv_flat,
    w_out_ref,
    b_out_flat,
    final_gain_flat,
    final_shift_flat,
    lists_ref,
    assignment_ref,
    columns_ref,
    out_ref,
    x_all,
    kv_all,
    w_qkv,
    w_out,
    normed,
    queries,
    attended,
    b_qkv_ref,
    vectors,
    local_sem,
    up_send,
    down_send,
    side_send,
    line_recv,
    side_recv,
    mate_sem,
):
    me = lax.axis_index("tm")
    side = lax.axis_index("space")
    other = 1 - side
    rows, width = x_ref.shape
    half_rows = rows // 2
    mate = me + 1 - 2 * lax.rem(me, 2)
    load_x = [
        pltpu.make_async_copy(
            x_ref.at[pl.ds(half * half_rows, half_rows)],
            x_all.at[me, side, half],
            local_sem.at[2 + half],
        )
        for half in range(2)
    ]
    load_qkv = pltpu.make_async_copy(w_qkv_ref, w_qkv, local_sem.at[0])
    load_out = pltpu.make_async_copy(w_out_ref, w_out, local_sem.at[1])
    for load in load_x:
        load.start()
    load_qkv.start()
    load_out.start()

    has_up = me < times - 1
    has_down = me > 0

    barrier = pltpu.get_barrier_semaphore()
    pl.semaphore_signal(barrier, inc=1, device_id={"space": other}, device_id_type=MESH)

    @pl.when(has_up)
    def _():
        pl.semaphore_signal(barrier, inc=1, device_id={"tm": me + 1}, device_id_type=MESH)

    @pl.when(has_down)
    def _():
        pl.semaphore_signal(barrier, inc=1, device_id={"tm": me - 1}, device_id_type=MESH)

    pl.semaphore_wait(barrier, 1 + has_up.astype(jnp.int32) + has_down.astype(jnp.int32))

    def up_copy(source, block, half):
        return pltpu.make_async_remote_copy(
            source, x_all.at[block, side, half], up_send.at[block, half],
            line_recv.at[block, half], device_id={"tm": me + 1}, device_id_type=MESH,
        )

    def down_copy(source, block, half):
        return pltpu.make_async_remote_copy(
            source, x_all.at[block, side, half], down_send.at[block, half],
            line_recv.at[block, half], device_id={"tm": me - 1}, device_id_type=MESH,
        )

    def side_copy(block, half, from_side, source=None):
        place = x_all.at[block, from_side, half]
        return pltpu.make_async_remote_copy(
            place if source is None else source, place, side_send.at[block, half],
            side_recv.at[block, half], device_id={"space": other}, device_id_type=MESH,
        )

    def mate_copy(block):
        place = x_all.at[block, other, 1]
        return pltpu.make_async_remote_copy(
            place, place, mate_sem.at[0], mate_sem.at[1],
            device_id={"tm": mate}, device_id_type=MESH,
        )

    for half in range(2):
        own_half = x_ref.at[pl.ds(half * half_rows, half_rows)]

        @pl.when(has_up)
        def _():
            up_copy(own_half, me, half).start()

        @pl.when(has_down)
        def _():
            down_copy(own_half, me, half).start()

        side_copy(me, half, side, own_half).start()

    b_qkv_ref[...] = b_qkv_flat[...].reshape(1, 3 * width)
    flats = (gain_flat, shift_flat, b_out_flat, final_gain_flat, final_shift_flat)
    for place, flat in enumerate(flats):
        vectors[place : place + 1, :] = flat[...].reshape(1, width)
    gain_ref, shift_ref, b_out_ref, final_gain_ref, final_shift_ref = (
        vectors.at[place : place + 1, :] for place in range(len(flats))
    )

    def send_aside(block, half):
        if half == 0:
            side_copy(block, half, side).start()
        else:

            @pl.when(block != mate)
            def _():
                side_copy(block, half, side).start()

    def arrive_and_forward(step, half):
        below, above = me - step, me + step

        @pl.when(below >= 0)
        def _():
            held = x_all.at[below, side, half]
            up_copy(held, below, half).wait_recv()

            @pl.when(has_up)
            def _():
                up_copy(held, below, half).start()

            send_aside(below, half)

        @pl.when(above < times)
        def _():
            held = x_all.at[above, side, half]
            down_copy(held, above, half).wait_recv()

            @pl.when(has_down)
            def _():
                down_copy(held, above, half).start()

            send_aside(above, half)

    reach = jnp.minimum(me, times - 1 - me)
    toward = mate - me

    def ordered(place):
        if place == 0:
            return me
        near = me + ((place + 1) // 2) * (toward if place % 2 else -toward)
        far_step = place - reach
        far = jnp.where(2 * me > times - 1, me - far_step, me + far_step)
        return jnp.where(place <= 2 * reach, near, far)

    tiles = 2 * width // WINDOW

    def project(pieces):
        count = len(pieces)
        for place, (block, from_side, half) in enumerate(pieces):
            normed[place * half_rows : (place + 1) * half_rows, :] = norm_rows(
                x_all[block, from_side, half], gain_ref[...], shift_ref[...]
            )

        def one_tile(tile, carried):
            start = pl.multiple_of(tile * WINDOW, WINDOW)
            shifted = pl.multiple_of(width + tile * WINDOW, LANES)
            made = jnp.dot(
                normed[: count * half_rows, :],
                w_qkv[:, pl.ds(shifted, WINDOW)],
                preferred_element_type=jnp.float32,
            )
            made = (made + b_qkv_ref[:, pl.ds(shifted, WINDOW)]).astype(jnp.bfloat16)
            for place, (block, from_side, half) in enumerate(pieces):
                kv_all[block * 2 + from_side, half, :, pl.ds(start, WINDOW)] = made[
                    place * half_rows : (place + 1) * half_rows, :
                ]
            return carried

        lax.fori_loop(0, tiles, one_tile, 0)

    def from_aside(place):
        block = ordered(place)
        pieces = []
        for half in range(1 if place == 1 else 2):
            side_copy(block, half, other).wait_recv()
            pieces.append((block, other, half))
        return pieces

    for load in load_x:
        load.wait()
    load_qkv.wait()
    project([(me, side, 0), (me, side, 1)])
    last = ordered(times - 1)
    for step in range(1, times - 1):
        arrive_and_forward(step, 0)
        arrive_and_forward(step, 1)
        ready = from_aside(step - 1)
        if step == times - 2:
            mate_copy(me).start()
        project([(ordered(step), side, 0), (ordered(step), side, 1)] + ready)
    arrive_and_forward(times - 1, 0)
    project([(last, side, 0)] + from_aside(times - 2))
    arrive_and_forward(times - 1, 1)
    side_copy(last, 0, other).wait_recv()
    project([(last, side, 1), (last, other, 0)])
    side_copy(last, 1, other).wait_recv()
    mate_copy(mate).wait_recv()
    project([(last, other, 1), (mate, other, 1)])

    owner = assignment_ref[me * 2 + side]
    list_places = lax.broadcasted_iota(jnp.int32, lists_ref.shape, 0)
    lists = lists_ref[...].astype(jnp.float32)
    token_row = jnp.sum(jnp.where(list_places == owner, lists, 0.0), axis=0, keepdims=True)
    capacity = lists_ref.shape[1]
    diagonal = lax.broadcasted_iota(jnp.int32, (capacity, capacity), 0) == lax.broadcasted_iota(
        jnp.int32, (capacity, capacity), 1
    )
    tokens = jnp.sum(jnp.where(diagonal, token_row, 0.0), axis=1, keepdims=True)
    one_hot = (tokens == columns_ref[...]).astype(jnp.float32).astype(jnp.bfloat16)
    picked = jnp.dot(
        one_hot,
        x_all[...].reshape(times * 2 * rows, width),
        preferred_element_type=jnp.float32,
    )
    out_ref[0] = picked.astype(jnp.bfloat16)
    queries[...] = (
        jnp.dot(
            norm_rows(picked, gain_ref[...], shift_ref[...]),
            w_qkv[:, :width],
            preferred_element_type=jnp.float32,
        )
        + b_qkv_ref[:, :width]
    ).astype(jnp.bfloat16)
    attended[...] = jnp.zeros_like(attended)
    score_scale = math.log2(math.e) / math.sqrt(head_width)
    all_rows = times * 2 * rows

    def window_of(first):
        return min(first // LANES, width // LANES - 2) * LANES

    groups = []
    head = 0
    while head < HEADS:
        base = window_of(head * head_width)
        count = 1
        while head + count < HEADS and (head + count + 1) * head_width <= base + WINDOW:
            count += 1
        groups.append((base, range(head, head + count)))
        head += count

    for base, heads in groups:
        lane = lax.broadcasted_iota(jnp.int32, (capacity, WINDOW), 1) + base
        inside = [(lane >= h * head_width) & (lane < (h + 1) * head_width) for h in heads]
        window_queries = queries[:, base : base + WINDOW].astype(jnp.float32)
        query = jnp.concatenate(
            [jnp.where(mask, window_queries, 0.0).astype(jnp.bfloat16) for mask in inside]
        )
        keys = kv_all[:, :, :, base : base + WINDOW].reshape(all_rows, WINDOW)
        values = kv_all[:, :, :, width + base : width + base + WINDOW].reshape(all_rows, WINDOW)
        scores = (
            lax.dot_general(
                query, keys, (((1,), (1,)), ((), ())), preferred_element_type=jnp.float32
            )
            * score_scale
        )
        weights = jnp.exp2(scores - jnp.max(scores, axis=1, keepdims=True))
        totals = jnp.sum(weights, axis=1, keepdims=True)
        summed = jnp.dot(weights.astype(jnp.bfloat16), values, preferred_element_type=jnp.float32)
        summed = summed / totals
        for place, mask in enumerate(inside):
            attended[:, base : base + WINDOW] += jnp.where(
                mask, summed[place * capacity : (place + 1) * capacity], 0.0
            )

    load_out.wait()
    hidden = (
        out_ref[0].astype(jnp.float32)
        + jnp.dot(
            attended[...].astype(jnp.bfloat16), w_out[...], preferred_element_type=jnp.float32
        )
        + b_out_ref[...]
    ).astype(jnp.bfloat16)
    final = layer_norm(hidden.astype(jnp.float32), final_gain_ref[...], final_shift_ref[...])
    out_ref[0] = jnp.where(tokens >= 0, final, 0.0).astype(jnp.bfloat16)

    for block in range(times):
        for half in range(2):

            @pl.when(has_up & (block <= me))
            def _():
                up_copy(x_all.at[block, side, half], block, half).wait_send()

            @pl.when(has_down & (block >= me))
            def _():
                down_copy(x_all.at[block, side, half], block, half).wait_send()

            @pl.when((block != mate) | (half == 0))
            def _():
                side_copy(block, half, side).wait_send()

    mate_copy(me).wait_send()


def fits_fused(times, spaces, rows, width, capacity):
    all_rows = times * spaces * rows
    held = 2 * (all_rows * width * 3 + width * width * 4 + 2 * rows * width)
    held += 4 * capacity * (width * 2 + all_rows * 3)
    return (
        spaces == 2
        and held < VMEM_LIMIT
        and width % LANES == 0
        and width // HEADS <= LANES
        and rows % 32 == 0
        and times % 2 == 0
        and times > 2
    )


def fused_local(
    activations,
    attn_gain,
    attn_shift,
    w_qkv,
    b_qkv,
    w_out,
    b_out,
    final_gain,
    final_shift,
    mask_tokens,
    assignment,
):
    frames, patches, width = activations.shape
    rows = frames * patches
    times = lax.axis_size("tm")
    spaces = lax.axis_size("space")
    if not fits_fused(times, spaces, rows, width, mask_tokens.shape[1]):
        return local(
            activations, attn_gain, attn_shift, w_qkv, b_qkv, w_out, b_out,
            final_gain, final_shift, mask_tokens, assignment,
        )
    capacity = mask_tokens.shape[1]
    order = np.arange(times * frames * spaces * patches).reshape(times, frames, spaces, patches)
    columns = order.transpose(0, 2, 1, 3).reshape(1, -1).astype(np.float32)
    vmem = pl.BlockSpec(memory_space=pltpu.VMEM)
    hbm = pl.BlockSpec(memory_space=pl.ANY)
    smem = pl.BlockSpec(memory_space=pltpu.SMEM)
    return pl.pallas_call(
        functools.partial(fused_kernel, times, width // HEADS),
        out_shape=jax.ShapeDtypeStruct((1, capacity, width), jnp.bfloat16),
        in_specs=[vmem, vmem, vmem, hbm, vmem, hbm, vmem, vmem, vmem, vmem, smem, vmem],
        out_specs=vmem,
        scratch_shapes=[
            pltpu.VMEM((times, spaces, 2, rows // 2, width), jnp.bfloat16),
            pltpu.VMEM((times * spaces, 2, rows // 2, 2 * width), jnp.bfloat16),
            pltpu.VMEM(w_qkv.shape, jnp.bfloat16),
            pltpu.VMEM(w_out.shape, jnp.bfloat16),
            pltpu.VMEM((2 * rows, width), jnp.bfloat16),
            pltpu.VMEM((capacity, width), jnp.bfloat16),
            pltpu.VMEM((capacity, width), jnp.float32),
            pltpu.VMEM((1, 3 * width), jnp.float32),
            pltpu.VMEM((5, width), jnp.float32),
            pltpu.SemaphoreType.DMA((4,)),
            pltpu.SemaphoreType.DMA((times, 2)),
            pltpu.SemaphoreType.DMA((times, 2)),
            pltpu.SemaphoreType.DMA((times, 2)),
            pltpu.SemaphoreType.DMA((times, 2)),
            pltpu.SemaphoreType.DMA((times, 2)),
            pltpu.SemaphoreType.DMA((2,)),
        ],
        compiler_params=pltpu.CompilerParams(
            collective_id=0, has_side_effects=True, vmem_limit_bytes=VMEM_LIMIT
        ),
    )(
        activations.reshape(rows, width),
        attn_gain,
        attn_shift,
        w_qkv,
        b_qkv,
        w_out,
        b_out,
        final_gain,
        final_shift,
        mask_tokens,
        assignment,
        jnp.asarray(columns),
    )


def solution(mesh):
    in_specs = (
        P(("clip", "tm"), "space", None),
        P(),
        P(),
        P(),
        P(),
        P(),
        P(),
        P(),
        P(),
        P("clip", None),
        P("clip"),
    )
    out_specs = P(("clip", "tm", "space"), None, None)
    return jax.shard_map(fused_local, mesh=mesh, in_specs=in_specs, out_specs=out_specs, check_vma=False)
```

```python
import functools
import math

import jax
import jax.numpy as jnp
import numpy as np
from jax import lax
from jax.experimental import pallas as pl
from jax.experimental.pallas import tpu as pltpu
from jax.sharding import PartitionSpec as P

HEADS = 16


EPSILON = 1e-06
FLOOR_SCORE = -1e30


def layer_norm(values, ln_gain, ln_shift):
    centre = jnp.mean(values, axis=-1, keepdims=True)
    deviation = values - centre
    variance = jnp.mean(deviation * deviation, axis=-1, keepdims=True)
    return deviation * lax.rsqrt(variance + EPSILON) * ln_gain + ln_shift


def start_state(query_heads):
    query_count, head_count, head_width = query_heads.shape
    return (
        jnp.full((head_count, query_count), FLOOR_SCORE, jnp.float32),
        jnp.zeros((head_count, query_count), jnp.float32),
        jnp.zeros((head_count, query_count, head_width), jnp.float32),
    )


def finish_state(carried_state):
    running_max, running_total, running_sum = carried_state
    return jnp.transpose(running_sum / running_total[:, :, None], (1, 0, 2)).astype(jnp.bfloat16)


def make_attend(query_heads):
    query_count, head_count, head_width = query_heads.shape
    score_scale = 1.0 / math.sqrt(head_width)

    def one_block(carried_state, kv_block):
        running_max, running_total, running_sum = carried_state
        block_length = kv_block.shape[1]
        key_rows = kv_block[0].reshape(block_length, head_count, head_width)
        value_rows = kv_block[1].reshape(block_length, head_count, head_width)
        scores = (
            jnp.einsum("qhe,khe->hqk", query_heads, key_rows, preferred_element_type=jnp.float32)
            * score_scale
        )
        new_max = jnp.maximum(running_max, jnp.max(scores, axis=-1))
        factor = jnp.exp(running_max - new_max)
        weights = jnp.exp(scores - new_max[:, :, None])
        running_total = running_total * factor + jnp.sum(weights, axis=-1)
        running_sum = running_sum * factor[:, :, None] + jnp.einsum(
            "hqk,khe->hqe",
            weights.astype(jnp.bfloat16),
            value_rows,
            preferred_element_type=jnp.float32,
        )
        return (new_max, running_total, running_sum)

    def attend(carried_state, key_piece, first_row):
        length = key_piece.shape[1]
        block_rows = length
        while block_rows > 1024 and block_rows % 2 == 0:
            block_rows = block_rows // 2

        def advance(position, carried):
            kv_block = lax.dynamic_slice_in_dim(key_piece, position * block_rows, block_rows, 1)
            return one_block(carried, kv_block)

        return lax.fori_loop(0, length // block_rows, advance, carried_state)

    return attend


def local(
    activations,
    attn_gain,
    attn_shift,
    w_qkv,
    b_qkv,
    w_out,
    b_out,
    final_gain,
    final_shift,
    mask_tokens,
    assignment,
):
    frame_count, patch_count, model_width = activations.shape
    local_rows = frame_count * patch_count
    head_width = model_width // HEADS
    tokens_flat = activations.reshape(local_rows, model_width)
    normed_in = layer_norm(tokens_flat.astype(jnp.float32), attn_gain, attn_shift).astype(
        jnp.bfloat16
    )
    projected = (jnp.dot(normed_in, w_qkv, preferred_element_type=jnp.float32) + b_qkv).astype(
        jnp.bfloat16
    )
    query_rows = projected[:, :model_width]
    paired = jnp.stack(
        (projected[:, model_width : 2 * model_width], projected[:, 2 * model_width :])
    )
    groups = lax.axis_size("space")
    group_heads = HEADS // groups
    stacked = jnp.stack((query_rows, paired[0], paired[1])).reshape(
        3, local_rows, groups, group_heads, head_width
    )
    swapped = lax.all_to_all(stacked, "space", split_axis=2, concat_axis=1, tiled=True)
    gathered_rows = swapped.shape[1]
    kept_heads = swapped.shape[3]
    query_heads = swapped[0].reshape(gathered_rows, kept_heads, head_width)
    kv_rows = swapped[1:].reshape(2, gathered_rows, kept_heads * head_width)
    time_state = make_attend(query_heads)(
        start_state(query_heads), lax.all_gather(kv_rows, "tm", axis=1, tiled=True), jnp.int32(0)
    )
    head_output = finish_state(time_state).reshape(gathered_rows, 1, kept_heads, head_width)
    merged = lax.all_to_all(head_output, "space", split_axis=0, concat_axis=1, tiled=True)
    attended = merged.reshape(local_rows, model_width)
    hidden = (
        tokens_flat.astype(jnp.float32)
        + jnp.dot(attended, w_out, preferred_element_type=jnp.float32)
        + b_out
    ).astype(jnp.bfloat16)
    normed = layer_norm(hidden.astype(jnp.float32), final_gain, final_shift).astype(jnp.bfloat16)
    owners = mask_tokens.shape[0]
    capacity = mask_tokens.shape[1]
    per_source = capacity // owners
    spaces = lax.axis_size("space")
    spatial = patch_count * spaces
    own_index = lax.axis_index("tm") * spaces + lax.axis_index("space")
    owner_lists = jnp.take(mask_tokens, assignment, axis=0)
    listed = owner_lists >= 0
    clipped = jnp.maximum(owner_lists, 0)
    token_frame = clipped // spatial
    token_patch = clipped % spatial
    home_device = token_frame // frame_count * spaces + token_patch // patch_count
    local_row = token_frame % frame_count * patch_count + token_patch % patch_count
    mine = listed & (home_device == own_index)
    slot_index = jnp.cumsum(mine.astype(jnp.int32), axis=1) - 1
    wanted = mine[:, None, :] & (
        slot_index[:, None, :] == jnp.arange(per_source, dtype=jnp.int32)[None, :, None]
    )
    picks = jnp.sum(jnp.where(wanted, local_row[:, None, :], 0), axis=-1)
    present = jnp.any(wanted, axis=-1)
    own_home = lax.dynamic_index_in_dim(home_device, own_index, 0, keepdims=False)
    own_listed = lax.dynamic_index_in_dim(listed, own_index, 0, keepdims=False)
    entry_order = jnp.arange(capacity, dtype=jnp.int32)
    earlier = (
        (entry_order[:, None] < entry_order[None, :])
        & own_listed[:, None]
        & (own_home[:, None] == own_home[None, :])
    )
    entry_rank = jnp.sum(earlier.astype(jnp.int32), axis=0)
    where_from = jnp.where(own_listed, own_home * per_source + entry_rank, 0)
    outgoing = jnp.where(
        present[:, :, None], jnp.take(normed, picks, axis=0), jnp.zeros((), jnp.bfloat16)
    )
    arrived = lax.all_to_all(outgoing, ("tm", "space"), split_axis=0, concat_axis=0, tiled=True)
    row_table = arrived.reshape(owners * per_source, model_width)
    placed = jnp.take(row_table, where_from, axis=0)
    return jnp.where(own_listed[:, None], placed, jnp.zeros((), jnp.bfloat16))[None]


LANES = 128
WINDOW = 256
VMEM_LIMIT = 60 * 1024 * 1024
MESH = pl.DeviceIdType.MESH


def norm_rows(values, gain, shift):
    return layer_norm(values.astype(jnp.float32), gain, shift).astype(jnp.bfloat16)


def fused_kernel(
    times,
    head_width,
    x_ref,
    gain_flat,
    shift_flat,
    w_qkv_ref,
    b_qkv_flat,
    w_out_ref,
    b_out_flat,
    final_gain_flat,
    final_shift_flat,
    lists_ref,
    assignment_ref,
    columns_ref,
    out_ref,
    x_all,
    kv_all,
    w_qkv,
    w_out,
    normed,
    queries,
    attended,
    b_qkv_ref,
    vectors,
    local_sem,
    up_send,
    down_send,
    side_send,
    line_recv,
    side_recv,
    mate_sem,
):
    me = lax.axis_index("tm")
    side = lax.axis_index("space")
    other = 1 - side
    rows, width = x_ref.shape
    half_rows = rows // 2
    mate = me + 1 - 2 * lax.rem(me, 2)
    load_x = [
        pltpu.make_async_copy(
            x_ref.at[pl.ds(half * half_rows, half_rows)],
            x_all.at[me, side, half],
            local_sem.at[2 + half],
        )
        for half in range(2)
    ]
    load_qkv = pltpu.make_async_copy(w_qkv_ref, w_qkv, local_sem.at[0])
    load_out = pltpu.make_async_copy(w_out_ref, w_out, local_sem.at[1])
    for load in load_x:
        load.start()
    load_qkv.start()
    load_out.start()

    has_up = me < times - 1
    has_down = me > 0

    barrier = pltpu.get_barrier_semaphore()
    pl.semaphore_signal(barrier, inc=1, device_id={"space": other}, device_id_type=MESH)

    @pl.when(has_up)
    def _():
        pl.semaphore_signal(barrier, inc=1, device_id={"tm": me + 1}, device_id_type=MESH)

    @pl.when(has_down)
    def _():
        pl.semaphore_signal(barrier, inc=1, device_id={"tm": me - 1}, device_id_type=MESH)

    pl.semaphore_wait(barrier, 1 + has_up.astype(jnp.int32) + has_down.astype(jnp.int32))

    def up_copy(source, block, half):
        return pltpu.make_async_remote_copy(
            source, x_all.at[block, side, half], up_send.at[block, half],
            line_recv.at[block, half], device_id={"tm": me + 1}, device_id_type=MESH,
        )

    def down_copy(source, block, half):
        return pltpu.make_async_remote_copy(
            source, x_all.at[block, side, half], down_send.at[block, half],
            line_recv.at[block, half], device_id={"tm": me - 1}, device_id_type=MESH,
        )

    def side_copy(block, half, from_side, source=None):
        place = x_all.at[block, from_side, half]
        return pltpu.make_async_remote_copy(
            place if source is None else source, place, side_send.at[block, half],
            side_recv.at[block, half], device_id={"space": other}, device_id_type=MESH,
        )

    def mate_copy(block):
        place = x_all.at[block, other, 1]
        return pltpu.make_async_remote_copy(
            place, place, mate_sem.at[0], mate_sem.at[1],
            device_id={"tm": mate}, device_id_type=MESH,
        )

    for half in range(2):
        own_half = x_ref.at[pl.ds(half * half_rows, half_rows)]

        @pl.when(has_up)
        def _():
            up_copy(own_half, me, half).start()

        @pl.when(has_down)
        def _():
            down_copy(own_half, me, half).start()

        side_copy(me, half, side, own_half).start()

    b_qkv_ref[...] = b_qkv_flat[...].reshape(1, 3 * width)
    flats = (gain_flat, shift_flat, b_out_flat, final_gain_flat, final_shift_flat)
    for place, flat in enumerate(flats):
        vectors[place : place + 1, :] = flat[...].reshape(1, width)
    gain_ref, shift_ref, b_out_ref, final_gain_ref, final_shift_ref = (
        vectors.at[place : place + 1, :] for place in range(len(flats))
    )

    def send_aside(block, half):
        if half == 0:
            side_copy(block, half, side).start()
        else:

            @pl.when(block != mate)
            def _():
                side_copy(block, half, side).start()

    def arrive_and_forward(step, half):
        below, above = me - step, me + step

        @pl.when(below >= 0)
        def _():
            held = x_all.at[below, side, half]
            up_copy(held, below, half).wait_recv()

            @pl.when(has_up)
            def _():
                up_copy(held, below, half).start()

            send_aside(below, half)

        @pl.when(above < times)
        def _():
            held = x_all.at[above, side, half]
            down_copy(held, above, half).wait_recv()

            @pl.when(has_down)
            def _():
                down_copy(held, above, half).start()

            send_aside(above, half)

    reach = jnp.minimum(me, times - 1 - me)
    toward = mate - me

    def ordered(place):
        if place == 0:
            return me
        near = me + ((place + 1) // 2) * (toward if place % 2 else -toward)
        far_step = place - reach
        far = jnp.where(2 * me > times - 1, me - far_step, me + far_step)
        return jnp.where(place <= 2 * reach, near, far)

    tiles = 2 * width // WINDOW

    def project(pieces):
        count = len(pieces)
        for place, (block, from_side, half) in enumerate(pieces):
            normed[place * half_rows : (place + 1) * half_rows, :] = norm_rows(
                x_all[block, from_side, half], gain_ref[...], shift_ref[...]
            )

        def one_tile(tile, carried):
            start = pl.multiple_of(tile * WINDOW, WINDOW)
            shifted = pl.multiple_of(width + tile * WINDOW, LANES)
            made = jnp.dot(
                normed[: count * half_rows, :],
                w_qkv[:, pl.ds(shifted, WINDOW)],
                preferred_element_type=jnp.float32,
            )
            made = (made + b_qkv_ref[:, pl.ds(shifted, WINDOW)]).astype(jnp.bfloat16)
            for place, (block, from_side, half) in enumerate(pieces):
                kv_all[block * 2 + from_side, half, :, pl.ds(start, WINDOW)] = made[
                    place * half_rows : (place + 1) * half_rows, :
                ]
            return carried

        lax.fori_loop(0, tiles, one_tile, 0)

    def from_aside(place):
        block = ordered(place)
        pieces = []
        for half in range(1 if place == 1 else 2):
            side_copy(block, half, other).wait_recv()
            pieces.append((block, other, half))
        return pieces

    for load in load_x:
        load.wait()
    load_qkv.wait()
    project([(me, side, 0), (me, side, 1)])
    last = ordered(times - 1)
    for step in range(1, times - 1):
        arrive_and_forward(step, 0)
        arrive_and_forward(step, 1)
        ready = from_aside(step - 1)
        if step == times - 2:
            mate_copy(me).start()
        project([(ordered(step), side, 0), (ordered(step), side, 1)] + ready)
    arrive_and_forward(times - 1, 0)
    project([(last, side, 0)] + from_aside(times - 2))
    arrive_and_forward(times - 1, 1)
    side_copy(last, 0, other).wait_recv()
    project([(last, side, 1), (last, other, 0)])
    owner = assignment_ref[me * 2 + side]
    list_places = lax.broadcasted_iota(jnp.int32, lists_ref.shape, 0)
    lists = lists_ref[...].astype(jnp.float32)
    token_row = jnp.sum(jnp.where(list_places == owner, lists, 0.0), axis=0, keepdims=True)
    capacity = lists_ref.shape[1]
    diagonal = lax.broadcasted_iota(jnp.int32, (capacity, capacity), 0) == lax.broadcasted_iota(
        jnp.int32, (capacity, capacity), 1
    )
    tokens = jnp.sum(jnp.where(diagonal, token_row, 0.0), axis=1, keepdims=True)

    def pick(block, from_side):
        listed = tokens == columns_ref[pl.ds(block * 2 + from_side, 1), :]
        return jnp.dot(
            listed.astype(jnp.float32).astype(jnp.bfloat16),
            x_all[block, from_side].reshape(rows, width),
            preferred_element_type=jnp.float32,
        )

    picked = pick(0, side)
    for block in range(1, times):
        picked += pick(block, side)

    side_copy(last, 1, other).wait_recv()
    mate_copy(mate).wait_recv()
    project([(last, other, 1), (mate, other, 1)])

    for block in range(times):
        picked += pick(block, other)
    out_ref[0] = picked.astype(jnp.bfloat16)
    queries[...] = (
        jnp.dot(
            norm_rows(picked, gain_ref[...], shift_ref[...]),
            w_qkv[:, :width],
            preferred_element_type=jnp.float32,
        )
        + b_qkv_ref[:, :width]
    ).astype(jnp.bfloat16)
    attended[...] = jnp.zeros_like(attended)
    score_scale = math.log2(math.e) / math.sqrt(head_width)
    all_rows = times * 2 * rows

    def window_of(first):
        return min(first // LANES, width // LANES - 2) * LANES

    groups = []
    head = 0
    while head < HEADS:
        base = window_of(head * head_width)
        count = 1
        while head + count < HEADS and (head + count + 1) * head_width <= base + WINDOW:
            count += 1
        groups.append((base, range(head, head + count)))
        head += count

    for base, heads in groups:
        lane = lax.broadcasted_iota(jnp.int32, (capacity, WINDOW), 1) + base
        inside = [(lane >= h * head_width) & (lane < (h + 1) * head_width) for h in heads]
        window_queries = queries[:, base : base + WINDOW].astype(jnp.float32)
        query = jnp.concatenate(
            [jnp.where(mask, window_queries, 0.0).astype(jnp.bfloat16) for mask in inside]
        )
        keys = kv_all[:, :, :, base : base + WINDOW].reshape(all_rows, WINDOW)
        values = kv_all[:, :, :, width + base : width + base + WINDOW].reshape(all_rows, WINDOW)
        scores = (
            lax.dot_general(
                query, keys, (((1,), (1,)), ((), ())), preferred_element_type=jnp.float32
            )
            * score_scale
        )
        weights = jnp.exp2(scores - jnp.max(scores, axis=1, keepdims=True))
        totals = jnp.sum(weights, axis=1, keepdims=True)
        summed = jnp.dot(weights.astype(jnp.bfloat16), values, preferred_element_type=jnp.float32)
        summed = summed / totals
        for place, mask in enumerate(inside):
            attended[:, base : base + WINDOW] += jnp.where(
                mask, summed[place * capacity : (place + 1) * capacity], 0.0
            )

    load_out.wait()
    hidden = (
        out_ref[0].astype(jnp.float32)
        + jnp.dot(
            attended[...].astype(jnp.bfloat16), w_out[...], preferred_element_type=jnp.float32
        )
        + b_out_ref[...]
    ).astype(jnp.bfloat16)
    final = layer_norm(hidden.astype(jnp.float32), final_gain_ref[...], final_shift_ref[...])
    out_ref[0] = jnp.where(tokens >= 0, final, 0.0).astype(jnp.bfloat16)

    for block in range(times):
        for half in range(2):

            @pl.when(has_up & (block <= me))
            def _():
                up_copy(x_all.at[block, side, half], block, half).wait_send()

            @pl.when(has_down & (block >= me))
            def _():
                down_copy(x_all.at[block, side, half], block, half).wait_send()

            @pl.when((block != mate) | (half == 0))
            def _():
                side_copy(block, half, side).wait_send()

    mate_copy(me).wait_send()


def fits_fused(times, spaces, rows, width, capacity):
    all_rows = times * spaces * rows
    held = 2 * (all_rows * width * 3 + width * width * 4 + 2 * rows * width)
    held += 4 * capacity * (width * 2 + all_rows * 3)
    return (
        spaces == 2
        and held < VMEM_LIMIT
        and width % LANES == 0
        and width // HEADS <= LANES
        and rows % 32 == 0
        and times % 2 == 0
        and times > 2
    )


def fused_local(
    activations,
    attn_gain,
    attn_shift,
    w_qkv,
    b_qkv,
    w_out,
    b_out,
    final_gain,
    final_shift,
    mask_tokens,
    assignment,
):
    frames, patches, width = activations.shape
    rows = frames * patches
    times = lax.axis_size("tm")
    spaces = lax.axis_size("space")
    if not fits_fused(times, spaces, rows, width, mask_tokens.shape[1]):
        return local(
            activations, attn_gain, attn_shift, w_qkv, b_qkv, w_out, b_out,
            final_gain, final_shift, mask_tokens, assignment,
        )
    capacity = mask_tokens.shape[1]
    order = np.arange(times * frames * spaces * patches).reshape(times, frames, spaces, patches)
    columns = order.transpose(0, 2, 1, 3).reshape(times * spaces, -1).astype(np.float32)
    vmem = pl.BlockSpec(memory_space=pltpu.VMEM)
    hbm = pl.BlockSpec(memory_space=pl.ANY)
    smem = pl.BlockSpec(memory_space=pltpu.SMEM)
    return pl.pallas_call(
        functools.partial(fused_kernel, times, width // HEADS),
        out_shape=jax.ShapeDtypeStruct((1, capacity, width), jnp.bfloat16),
        in_specs=[vmem, vmem, vmem, hbm, vmem, hbm, vmem, vmem, vmem, vmem, smem, vmem],
        out_specs=vmem,
        scratch_shapes=[
            pltpu.VMEM((times, spaces, 2, rows // 2, width), jnp.bfloat16),
            pltpu.VMEM((times * spaces, 2, rows // 2, 2 * width), jnp.bfloat16),
            pltpu.VMEM(w_qkv.shape, jnp.bfloat16),
            pltpu.VMEM(w_out.shape, jnp.bfloat16),
            pltpu.VMEM((2 * rows, width), jnp.bfloat16),
            pltpu.VMEM((capacity, width), jnp.bfloat16),
            pltpu.VMEM((capacity, width), jnp.float32),
            pltpu.VMEM((1, 3 * width), jnp.float32),
            pltpu.VMEM((5, width), jnp.float32),
            pltpu.SemaphoreType.DMA((4,)),
            pltpu.SemaphoreType.DMA((times, 2)),
            pltpu.SemaphoreType.DMA((times, 2)),
            pltpu.SemaphoreType.DMA((times, 2)),
            pltpu.SemaphoreType.DMA((times, 2)),
            pltpu.SemaphoreType.DMA((times, 2)),
            pltpu.SemaphoreType.DMA((2,)),
        ],
        compiler_params=pltpu.CompilerParams(
            collective_id=0, has_side_effects=True, vmem_limit_bytes=VMEM_LIMIT
        ),
    )(
        activations.reshape(rows, width),
        attn_gain,
        attn_shift,
        w_qkv,
        b_qkv,
        w_out,
        b_out,
        final_gain,
        final_shift,
        mask_tokens,
        assignment,
        jnp.asarray(columns),
    )


def solution(mesh):
    in_specs = (
        P(("clip", "tm"), "space", None),
        P(),
        P(),
        P(),
        P(),
        P(),
        P(),
        P(),
        P(),
        P("clip", None),
        P("clip"),
    )
    out_specs = P(("clip", "tm", "space"), None, None)
    return jax.shard_map(fused_local, mesh=mesh, in_specs=in_specs, out_specs=out_specs, check_vma=False)
```
